32 devices in a mesh: ctx: 4 (over x, core), chan: 8 (over z, y).
Axes of the slice: x: 2, y: 2, z: 4, core: 2. Of those that a mesh axis runs over, the one named last changes fastest.
Arguments:
- proj: bfloat16 [3, 1024, 4096], P(None, 'chan', 'ctx'), may hold values from -6 to 6
- taps: bfloat16 [3, 64, 128], replicated, may hold values from -0.5 to 0.5
- rate: float32 [1024, 16], P('chan'), may hold values from 0.00012207031 to 0.0333333333
- residue: float32 [1024, 16], P('chan'), may hold values from -6 to 6
- skip: float32 [1024], P('chan'), may hold values from -6 to 6
- out_weight: bfloat16 [1024, 1024], replicated, may hold values from -0.1875 to 0.1875
Outputs:
- output: bfloat16 [1024, 4096], P('chan', 'ctx')
The draws below stay inside these ranges and needn't reach their ends.
All inputs are finite; a program needn't handle non-finite values.
Results may differ from the reference program's by a relative error of at most 0.005.
Values may be sent and summed in bfloat16 or wider, within the bound.
A program may use at most 128 MiB of HBM per device.

```python
import math
import jax
import jax.numpy as jnp
from jax import lax

C = 1024
M = 16
GROUP = 16
TAPS = 128
LENGTH = 4096


def draw_rate(key, part):
    uniform_draw = jax.random.uniform(key, (C, M), jnp.float32)
    log_lowest = jnp.log(0.5 / LENGTH)
    return jnp.exp(log_lowest + (jnp.log(1.0 / 30.0) - log_lowest) * uniform_draw)


def level_of(key, dims, shards, least, largest):
    factor_of, own = 1.0, jax.random.fold_in(key, 6)
    for axis_at, parts in shards:
        steps = jnp.exp(jax.random.uniform(jax.random.fold_in(own, axis_at), (parts,), jnp.float32, least / len(shards), largest / len(shards)))
        factor_of = factor_of * jnp.repeat(steps, dims[axis_at] // parts).reshape([-1 if axis == axis_at else 1 for axis in range(len(dims))])
    return factor_of


def bell_draw(rng, shape, spread, bound, split=(), dtype=jnp.bfloat16):
    drawn = spread * jax.random.normal(rng, shape, jnp.float32)
    if split:
        drawn = drawn * level_of(rng, shape, split, -0.22, 0.18)
    return jnp.clip(drawn, -bound, bound).astype(dtype)


def setup_inputs(seed: int = 0) -> dict:
    key_of = jax.random.split(jax.random.key(seed), 7)
    proj = bell_draw(key_of[0], (3, C, LENGTH), 1.0, 6.0, ((1, 8), (2, 4)))
    taps = bell_draw(key_of[1], (3, C // GROUP, TAPS), TAPS ** -0.5, 0.5)
    rate = draw_rate(jax.random.fold_in(key_of[6], 71), 0)
    residue = bell_draw(key_of[3], (C, M), 1.0, 6.0, ((0, 8),), jnp.float32)
    skip = bell_draw(key_of[4], (C,), 1.0, 6.0, ((0, 8),), jnp.float32)
    out_weight = bell_draw(key_of[5], (C, C), C ** -0.5, 0.1875)
    return {"proj": proj, "taps": taps, "rate": rate, "residue": residue, "skip": skip, "out_weight": out_weight}


def reference(proj, taps, rate, residue, skip, out_weight):
    padded = jnp.pad(proj.astype(jnp.float32), ((0, 0), (0, 0), (TAPS - 1, 0)))
    kernel = jnp.repeat(taps.astype(jnp.float32), GROUP, axis=1)

    def add_tap(index, running):
        window = lax.dynamic_slice_in_dim(padded, (TAPS - 1 - index).astype(jnp.int32), LENGTH, 2)
        weight = lax.dynamic_slice_in_dim(kernel, index.astype(jnp.int32), 1, 2)
        return running + weight * window
    shorted = lax.fori_loop(0, TAPS, add_tap, jnp.zeros((3, C, LENGTH), jnp.float32))
    query_side = shorted[0]
    mixed = shorted[1] * shorted[2]
    residue_eff = residue * jnp.sqrt(2.0 * rate / M)
    positions = jnp.arange(LENGTH).astype(jnp.float32)
    group_size = math.gcd(C, 64)
    fft_len = 2 * LENGTH

    def one_group(packed):
        rate_group, residue_group, signal = packed
        filters = lax.optimization_barrier(jnp.sum(residue_group[:, :, None] * jnp.exp(-rate_group[:, :, None] * positions[None, None, :]), axis=1))
        product = jnp.fft.rfft(signal, n=fft_len) * jnp.fft.rfft(filters, n=fft_len)
        return jnp.fft.irfft(product, n=fft_len)[:, :LENGTH]
    longconv = lax.map(one_group, (rate.reshape(C // group_size, group_size, M), residue_eff.reshape(C // group_size, group_size, M), mixed.reshape(C // group_size, group_size, LENGTH))).reshape(C, LENGTH)
    gated = (query_side * (longconv + skip[:, None] * mixed)).astype(jnp.bfloat16)
    return jnp.dot(out_weight.T, gated, preferred_element_type=jnp.float32).astype(jnp.bfloat16)
```

```python
import functools
import jax
import jax.numpy as jnp
from jax import lax
from jax.experimental import pallas as pl
from jax.experimental.pallas import tpu as pltpu
from jax.sharding import PartitionSpec as P

GROUP = 16
BLOCK = 128


def lane_block(shape):
    return lax.broadcasted_iota(jnp.int32, shape, len(shape) - 1) // GROUP


def short_kernel(blocks, proj_ref, halo_ref, taps_ref, rate_ref, query_ref, mixed_ref, state_ref):
    groups = proj_ref.shape[1] // GROUP
    modes = rate_ref.shape[0]
    start = lax.axis_index("chan") * groups
    all_groups = taps_ref.shape[1]
    pick = (
        lax.broadcasted_iota(jnp.int32, (groups, all_groups), 1)
        == lax.broadcasted_iota(jnp.int32, (groups, all_groups), 0) + start
    ).astype(jnp.float32).astype(jnp.bfloat16)
    flip = (
        lax.broadcasted_iota(jnp.int32, (BLOCK, 2 * BLOCK), 1)
        == BLOCK - lax.broadcasted_iota(jnp.int32, (BLOCK, 2 * BLOCK), 0)
    ).astype(jnp.float32).astype(jnp.bfloat16)
    rows = []
    for stream in range(3):
        own = jnp.dot(pick, taps_ref[stream], preferred_element_type=jnp.float32)
        rows.append(
            jnp.dot(own.astype(jnp.bfloat16), flip, preferred_element_type=jnp.float32)
        )
    for g in range(groups):
        chans = slice(g * GROUP, (g + 1) * GROUP)
        outs = []
        for stream in range(3):
            wide = jnp.broadcast_to(rows[stream][g : g + 1, :], (BLOCK, 2 * BLOCK))
            band = pltpu.roll(wide, 0, 1, stride=1, stride_axis=0).astype(jnp.bfloat16)
            tiles = [
                proj_ref[stream, chans, b * BLOCK : (b + 1) * BLOCK] for b in range(blocks)
            ]
            now = jnp.concatenate(tiles, axis=0)
            before = jnp.concatenate([halo_ref[stream, chans, :]] + tiles[:-1], axis=0)
            signal = jnp.concatenate([before, now], axis=1)
            outs.append(
                lax.dot_general(
                    band, signal, (((1,), (1,)), ((), ())), preferred_element_type=jnp.float32
                )
            )
        query_ref[pl.ds(g, BLOCK, stride=groups), :] = outs[0]
        mixed_ref[pl.ds(g, BLOCK, stride=groups), :] = outs[1] * outs[2]
    decay = [jnp.exp(-rate_ref[m]) for m in range(modes)]

    def step(r, states):
        x = mixed_ref[pl.ds(pl.multiple_of(r * groups, groups), groups), :]
        return tuple(d * s + x for d, s in zip(decay, states))

    zero = jnp.zeros((groups, blocks * GROUP), jnp.float32)
    ends = lax.fori_loop(0, BLOCK, step, (zero,) * modes, unroll=8)
    at = lane_block(zero.shape)
    for m in range(modes):
        total, hop = ends[m], 1
        while hop < blocks:
            moved = jnp.exp(rate_ref[m] * (-float(BLOCK * hop))) * pltpu.roll(
                total, GROUP * hop, 1
            )
            total = total + jnp.where(at >= hop, moved, 0.0)
            hop *= 2
        state_ref[m] = total


def long_kernel(
    blocks, ctx, query_ref, mixed_ref, state_ref, ends_ref, rate_ref, residue_ref, skip_ref, gated_ref, work
):
    modes, groups = rate_ref.shape[0], rate_ref.shape[1]
    tokens = blocks * BLOCK
    index = lax.axis_index("ctx")
    shape = rate_ref.shape[1:]
    at = lane_block(shape)
    at_tokens = at.astype(jnp.float32) * float(BLOCK)
    entry, decay, weight = [], [], []
    for m in range(modes):
        rate = rate_ref[m]
        per_device = jnp.exp(rate * (-float(tokens)))
        incoming = jnp.zeros(shape, jnp.float32)
        for k in range(ctx):
            incoming = jnp.where(k < index, per_device * incoming + ends_ref[k, m], incoming)
        own = jnp.where(at >= 1, pltpu.roll(state_ref[m], GROUP, 1), 0.0)
        entry.append(own + jnp.exp(-rate * at_tokens) * incoming)
        decay.append(jnp.exp(-rate))
        weight.append(residue_ref[m] * jnp.sqrt(2.0 * rate / modes))
    skip = skip_ref[...]

    def step(r, states):
        where = pl.ds(pl.multiple_of(r * groups, groups), groups)
        x = mixed_ref[where, :]
        new = tuple(d * s + x for d, s in zip(decay, states))
        parts = [w * s for w, s in zip(weight, new)] + [skip * x]
        while len(parts) > 1:
            parts = [a + b for a, b in zip(parts[::2], parts[1::2])] + (
                [parts[-1]] if len(parts) % 2 else []
            )
        work[where, :] = query_ref[where, :] * parts[0]
        return new

    lax.fori_loop(0, BLOCK, step, tuple(entry), unroll=4)
    for g in range(groups):
        turned = work[pl.ds(g, BLOCK, stride=groups), :].T.astype(jnp.bfloat16)
        for b in range(blocks):
            gated_ref[g * GROUP : (g + 1) * GROUP, b * BLOCK : (b + 1) * BLOCK] = turned[
                b * GROUP : (b + 1) * GROUP
            ]


def per_device(ctx, proj, taps, rate, residue, skip, out_weight):
    width, tokens = proj.shape[1:]
    modes = rate.shape[1]
    groups, blocks = width // GROUP, tokens // BLOCK
    lanes = blocks * GROUP
    halo = lax.ppermute(
        proj[:, :, tokens - BLOCK :], "ctx", [(i, i + 1) for i in range(ctx - 1)]
    )

    def spread(value):
        return jnp.tile(value.reshape(groups, GROUP, modes).transpose(2, 0, 1), (1, 1, blocks))

    rate_l, residue_l = spread(rate), spread(residue)
    skip_l = jnp.tile(skip.reshape(groups, GROUP), (1, blocks))
    vmem = pl.BlockSpec(memory_space=pltpu.VMEM)
    major = jax.ShapeDtypeStruct((BLOCK * groups, lanes), jnp.float32)
    query, mixed, state = pl.pallas_call(
        functools.partial(short_kernel, blocks),
        out_shape=(major, major, jax.ShapeDtypeStruct((modes, groups, lanes), jnp.float32)),
        in_specs=[vmem] * 4,
        out_specs=(vmem,) * 3,
        compiler_params=pltpu.CompilerParams(vmem_limit_bytes=24 << 20),
        name="short",
    )(proj, halo, taps, rate_l)
    ends = lax.all_gather(state[:, :, lanes - GROUP :], "ctx")
    ends = jnp.tile(ends, (1, 1, 1, blocks))
    gated = pl.pallas_call(
        functools.partial(long_kernel, blocks, ctx),
        out_shape=jax.ShapeDtypeStruct((width, tokens), jnp.bfloat16),
        in_specs=[vmem] * 7,
        out_specs=vmem,
        scratch_shapes=[pltpu.VMEM(major.shape, jnp.float32)],
        compiler_params=pltpu.CompilerParams(vmem_limit_bytes=24 << 20),
        name="long",
    )(query, mixed, state, ends, rate_l, residue_l, skip_l)
    every = lax.all_gather(gated, "chan", axis=0, tiled=True)
    own = lax.dynamic_slice_in_dim(out_weight, lax.axis_index("chan") * width, width, 1)
    result = lax.dot_general(
        own, every, (((0,), (0,)), ((), ())), preferred_element_type=jnp.float32
    )
    return result.astype(jnp.bfloat16)


def solution(mesh):
    in_specs = (P(None, "chan", "ctx"), P(), P("chan", None), P("chan", None), P("chan"), P())
    out_specs = P("chan", "ctx")
    return jax.shard_map(
        functools.partial(per_device, mesh.shape["ctx"]),
        mesh=mesh,
        in_specs=in_specs,
        out_specs=out_specs,
        check_vma=False,
    )
```

```python
import functools
import jax
import jax.numpy as jnp
from jax import lax
from jax.experimental import pallas as pl
from jax.experimental.pallas import tpu as pltpu
from jax.sharding import PartitionSpec as P

GROUP = 16
BLOCK = 128
PIECES = 4
MESH = pl.DeviceIdType.MESH
HIGHEST = lax.Precision.HIGHEST


def iota(shape, axis):
    return lax.broadcasted_iota(jnp.int32, shape, axis)


def one_hot(hit, dtype=jnp.float32):
    return hit.astype(jnp.float32).astype(dtype)


def ring_place(chan, n):
    row, side = chan // 2, chan % 2
    return row + side * (n - 1 - 2 * row)


def ring_chan(place, n):
    side = place // (n // 2)
    row = place + side * (n - 1 - 2 * place)
    return 2 * row + side


def fused(
    ctx,
    chans,
    proj_ref,
    taps_ref,
    rate_ref,
    residue_ref,
    skip_ref,
    weight_ref,
    out_ref,
    halo,
    query,
    mixed,
    work,
    bands,
    rate_s,
    residue_s,
    state,
    ends,
    own_weight,
    gath,
    acc,
    weight_sem,
    halo_sems,
    end_send,
    end_recv,
    ring_send,
    ring_recv,
):
    width, tokens = proj_ref.shape[1:]
    modes = rate_ref.shape[1]
    groups, blocks = width // GROUP, tokens // BLOCK
    lanes = blocks * GROUP
    cols = tokens // PIECES
    index = lax.axis_index("ctx")
    chan = lax.axis_index("chan")
    place = ring_place(chan, chans)
    right = ring_chan((place + 1) % chans, chans)
    left = ring_chan((place + chans - 1) % chans, chans)

    barrier = pltpu.get_barrier_semaphore()
    for hop in range(1, ctx):
        pl.semaphore_signal(
            barrier, inc=1, device_id={"ctx": (index + hop) % ctx}, device_id_type=MESH
        )
    for peer in (left, right):
        pl.semaphore_signal(barrier, inc=1, device_id={"chan": peer}, device_id_type=MESH)

    if weight_ref.shape[1] == width:
        weight_from = weight_ref
    else:
        weight_from = weight_ref.at[:, pl.ds(pl.multiple_of(chan * width, width), width)]
    weight_copy = pltpu.make_async_copy(weight_from, own_weight, weight_sem)
    weight_copy.start()

    pl.semaphore_wait(barrier, ctx + 1)
    halo_copy = pltpu.make_async_remote_copy(
        src_ref=proj_ref.at[:, :, pl.ds(tokens - BLOCK, BLOCK)],
        dst_ref=halo,
        send_sem=halo_sems.at[0],
        recv_sem=halo_sems.at[1],
        device_id={"ctx": (index + 1) % ctx},
        device_id_type=MESH,
    )

    @pl.when(index < ctx - 1)
    def _():
        halo_copy.start()

    all_groups = taps_ref.shape[1]
    pick = one_hot(
        iota((groups, all_groups), 1) == iota((groups, all_groups), 0) + chan * groups,
        jnp.bfloat16,
    )
    flip = one_hot(
        iota((BLOCK, 2 * BLOCK), 1) == BLOCK - iota((BLOCK, 2 * BLOCK), 0), jnp.bfloat16
    )
    for stream in range(3):
        own = jnp.dot(pick, taps_ref[stream], preferred_element_type=jnp.float32)
        rows = jnp.dot(own.astype(jnp.bfloat16), flip, preferred_element_type=jnp.float32)
        for g in range(groups):
            wide = jnp.broadcast_to(rows[g : g + 1, :], (BLOCK, 2 * BLOCK))
            bands[stream, g] = pltpu.roll(wide, 0, 1, stride=1, stride_axis=0).astype(
                jnp.bfloat16
            )

    high = modes * groups
    expand = one_hot(iota((high, modes), 0) // groups == iota((high, modes), 1))
    kept = iota((high, width), 1) // GROUP == iota((high, width), 0) % groups
    spread = one_hot(iota((width, lanes), 0) % GROUP == iota((width, lanes), 1) % GROUP)

    def spread_rows(value):
        tall = lax.dot_general(
            expand,
            value,
            (((1,), (1,)), ((), ())),
            precision=HIGHEST,
            preferred_element_type=jnp.float32,
        )
        return jnp.dot(
            jnp.where(kept, tall, 0.0),
            spread,
            precision=HIGHEST,
            preferred_element_type=jnp.float32,
        )

    rate_s[...] = spread_rows(rate_ref[...])
    residue_s[...] = spread_rows(residue_ref[...]) * jnp.sqrt(2.0 * rate_s[...] / modes)
    skip_rows = jnp.where(
        iota((groups, width), 1) // GROUP == iota((groups, width), 0),
        jnp.broadcast_to(skip_ref[...], (groups, width)),
        0.0,
    )
    skip = jnp.dot(skip_rows, spread, precision=HIGHEST, preferred_element_type=jnp.float32)

    def of_mode(ref, m):
        return ref[m * groups : (m + 1) * groups, :]

    decay = [jnp.exp(-of_mode(rate_s, m)) for m in range(modes)]

    @pl.when(index > 0)
    def _():
        halo_copy.wait_recv()

    @pl.when(index == 0)
    def _():
        halo[...] = jnp.zeros_like(halo)

    def short(stream, g):
        rows_of = slice(g * GROUP, (g + 1) * GROUP)
        tiles = [proj_ref[stream, rows_of, b * BLOCK : (b + 1) * BLOCK] for b in range(blocks)]
        before = [halo[stream, rows_of, :]] + tiles[:-1]
        signal = jnp.concatenate(
            [jnp.concatenate(before, axis=0), jnp.concatenate(tiles, axis=0)], axis=1
        )
        return lax.dot_general(
            bands[stream, g], signal, (((1,), (1,)), ((), ())), preferred_element_type=jnp.float32
        )

    for g in range(groups):
        mixed[pl.ds(g, BLOCK, stride=groups), :] = short(1, g) * short(2, g)

    def gather_step(r, states):
        x = mixed[pl.ds(pl.multiple_of(r * groups, groups), groups), :]
        return tuple(d * s + x for d, s in zip(decay, states))

    zero = jnp.zeros((groups, lanes), jnp.float32)
    last = lax.fori_loop(0, BLOCK, gather_step, (zero,) * modes, unroll=8)
    at = iota(zero.shape, 1) // GROUP
    for m in range(modes):
        total, hop = last[m], 1
        while hop < blocks:
            moved = jnp.exp(of_mode(rate_s, m) * (-float(BLOCK * hop))) * pltpu.roll(
                total, GROUP * hop, 1
            )
            total = total + jnp.where(at >= hop, moved, 0.0)
            hop *= 2
        state[m * groups : (m + 1) * groups, :] = total

    end_copies = [
        pltpu.make_async_remote_copy(
            src_ref=state,
            dst_ref=ends.at[hop - 1],
            send_sem=end_send.at[hop - 1],
            recv_sem=end_recv.at[hop - 1],
            device_id={"ctx": (index + hop) % ctx},
            device_id_type=MESH,
        )
        for hop in range(1, ctx)
    ]
    for hop in range(1, ctx):

        @pl.when(index < ctx - hop)
        def _():
            end_copies[hop - 1].start()

    for g in range(groups):
        query[pl.ds(g, BLOCK, stride=groups), :] = short(0, g)

    for hop in range(1, ctx):

        @pl.when(index >= hop)
        def _():
            end_copies[hop - 1].wait_recv()

        @pl.when(index < hop)
        def _():
            ends[hop - 1] = jnp.zeros((high, lanes), jnp.float32)

    at_tokens = at.astype(jnp.float32) * float(BLOCK)
    entry, weight = [], []
    for m in range(modes):
        rate = of_mode(rate_s, m)
        per_device = jnp.exp(rate * (-float(tokens)))
        incoming = jnp.zeros_like(zero)
        for hop in range(ctx - 1, 0, -1):
            incoming = per_device * incoming + ends[hop - 1, m * groups : (m + 1) * groups, :]
        incoming = jnp.where(at == blocks - 1, incoming, 0.0)
        hop = 1
        while hop < blocks:
            incoming = incoming + pltpu.roll(incoming, GROUP * hop, 1)
            hop *= 2
        own = jnp.where(at >= 1, pltpu.roll(of_mode(state, m), GROUP, 1), 0.0)
        entry.append(own + jnp.exp(-rate * at_tokens) * incoming)
        weight.append(of_mode(residue_s, m))

    def step(r, states):
        where = pl.ds(pl.multiple_of(r * groups, groups), groups)
        x = mixed[where, :]
        new = tuple(d * s + x for d, s in zip(decay, states))
        parts = [w * s for w, s in zip(weight, new)] + [skip * x]
        while len(parts) > 1:
            parts = [a + b for a, b in zip(parts[::2], parts[1::2])] + (
                [parts[-1]] if len(parts) % 2 else []
            )
        work[where, :] = query[where, :] * parts[0]
        return new

    lax.fori_loop(0, BLOCK, step, tuple(entry), unroll=4)
    per_piece = blocks // PIECES
    for g in range(groups):
        turned = work[pl.ds(g, BLOCK, stride=groups), :].T.astype(jnp.bfloat16)
        for b in range(blocks):
            inside = (b % per_piece) * BLOCK
            gath[
                chan, b // per_piece, g * GROUP : (g + 1) * GROUP, inside : inside + BLOCK
            ] = turned[b * GROUP : (b + 1) * GROUP]

    half = chans // 2

    def ring_copy(way, hop, piece):
        shard = ring_chan((place + chans + (-hop if way == 0 else hop)) % chans, chans)
        return pltpu.make_async_remote_copy(
            src_ref=gath.at[shard, piece],
            dst_ref=gath.at[shard, piece],
            send_sem=ring_send.at[way, hop, piece],
            recv_sem=ring_recv.at[way, hop, piece],
            device_id={"chan": right if way == 0 else left},
            device_id_type=MESH,
        )

    def travels(way, hop, piece):
        if hop < half - 1:
            return True
        return hop == half - 1 and (piece < PIECES // 2) == (way == 0)

    copies = {}
    for piece in range(PIECES):
        for way in range(2):
            copies[way, 0, piece] = ring_copy(way, 0, piece)
            copies[way, 0, piece].start()
    weight_copy.wait()

    def project(shard, piece):
        rows_of = pl.ds(pl.multiple_of(shard * width, width), width)
        return lax.dot_general(
            own_weight[rows_of, :],
            gath[shard, piece],
            (((0,), (0,)), ((), ())),
            preferred_element_type=jnp.float32,
        )

    for piece in range(PIECES):
        acc[piece] = project(chan, piece)
    for hop in range(1, half + 1):
        for piece in range(PIECES):
            arrived = []
            for way in range(2):
                if not travels(way, hop - 1, piece):
                    continue
                copies[way, hop - 1, piece].wait_recv()
                if travels(way, hop, piece):
                    copies[way, hop, piece] = ring_copy(way, hop, piece)
                    copies[way, hop, piece].start()
                arrived.append(
                    ring_chan((place + chans + (-hop if way == 0 else hop)) % chans, chans)
                )
            total = acc[piece]
            for shard in arrived:
                total = total + project(shard, piece)
            if hop == half:
                out_ref[:, piece * cols : (piece + 1) * cols] = total.astype(out_ref.dtype)
            else:
                acc[piece] = total

    for key in copies:
        copies[key].wait_send()

    @pl.when(index < ctx - 1)
    def _():
        halo_copy.wait_send()

    for hop in range(1, ctx):

        @pl.when(index < ctx - hop)
        def _():
            end_copies[hop - 1].wait_send()


def per_device(ctx, chans, proj, taps, rate, residue, skip, out_weight):
    width, tokens = proj.shape[1:]
    modes = rate.shape[1]
    groups, blocks = width // GROUP, tokens // BLOCK
    lanes = blocks * GROUP
    if width % 128:
        out_weight = lax.dynamic_slice_in_dim(
            out_weight, lax.axis_index("chan") * width, width, 1
        )
    vmem = pl.BlockSpec(memory_space=pltpu.VMEM)
    major = pltpu.VMEM((BLOCK * groups, lanes), jnp.float32)
    table = pltpu.VMEM((modes * groups, lanes), jnp.float32)
    return pl.pallas_call(
        functools.partial(fused, ctx, chans),
        out_shape=jax.ShapeDtypeStruct((width, tokens), jnp.bfloat16),
        in_specs=[vmem] * 5 + [pl.BlockSpec(memory_space=pl.ANY)],
        out_specs=vmem,
        scratch_shapes=[
            pltpu.VMEM((3, width, BLOCK), jnp.bfloat16),
            major,
            major,
            major,
            pltpu.VMEM((3, groups, BLOCK, 2 * BLOCK), jnp.bfloat16),
            table,
            table,
            table,
            pltpu.VMEM((ctx - 1, modes * groups, lanes), jnp.float32),
            pltpu.VMEM((chans * width, width), jnp.bfloat16),
            pltpu.VMEM((chans, PIECES, width, tokens // PIECES), jnp.bfloat16),
            pltpu.VMEM((PIECES, width, tokens // PIECES), jnp.float32),
            pltpu.SemaphoreType.DMA,
            pltpu.SemaphoreType.DMA((2,)),
            pltpu.SemaphoreType.DMA((ctx - 1,)),
            pltpu.SemaphoreType.DMA((ctx - 1,)),
            pltpu.SemaphoreType.DMA((2, chans // 2, PIECES)),
            pltpu.SemaphoreType.DMA((2, chans // 2, PIECES)),
        ],
        compiler_params=pltpu.CompilerParams(
            vmem_limit_bytes=32 << 20, collective_id=0, has_side_effects=True
        ),
        name="fused",
    )(proj, taps, rate, residue, skip.reshape(1, width), out_weight)


def solution(mesh):
    in_specs = (P(None, "chan", "ctx"), P(), P("chan", None), P("chan", None), P("chan"), P())
    out_specs = P("chan", "ctx")
    return jax.shard_map(
        functools.partial(per_device, mesh.shape["ctx"], mesh.shape["chan"]),
        mesh=mesh,
        in_specs=in_specs,
        out_specs=out_specs,
        check_vma=False,
    )
```

```python
import functools
import jax
import jax.numpy as jnp
from jax import lax
from jax.experimental import pallas as pl
from jax.experimental.pallas import tpu as pltpu
from jax.sharding import PartitionSpec as P

GROUP = 16
BLOCK = 128
PIECES = 4
MESH = pl.DeviceIdType.MESH
HIGHEST = lax.Precision.HIGHEST


def iota(shape, axis):
    return lax.broadcasted_iota(jnp.int32, shape, axis)


def one_hot(hit, dtype=jnp.float32):
    return hit.astype(jnp.float32).astype(dtype)


def ring_place(chan, n):
    row, side = chan // 2, chan % 2
    return row + side * (n - 1 - 2 * row)


def ring_chan(place, n):
    side = place // (n // 2)
    row = place + side * (n - 1 - 2 * place)
    return 2 * row + side


def fused(
    ctx,
    chans,
    proj_in,
    taps_in,
    rate_in,
    residue_in,
    skip_in,
    weight_ref,
    out_ref,
    proj_ref,
    taps_ref,
    rate_ref,
    residue_ref,
    skip_ref,
    halo,
    query,
    mixed,
    work,
    bands,
    rate_s,
    residue_s,
    state,
    ends,
    own_weight,
    gath,
    acc,
    weight_sem,
    load_sems,
    halo_sems,
    end_send,
    end_recv,
    ring_send,
    ring_recv,
):
    width, tokens = proj_ref.shape[1:]
    modes = rate_ref.shape[0]
    groups, blocks = width // GROUP, tokens // BLOCK
    lanes = blocks * GROUP
    cols = tokens // PIECES
    index = lax.axis_index("ctx")
    chan = lax.axis_index("chan")
    place = ring_place(chan, chans)
    right = ring_chan((place + 1) % chans, chans)
    left = ring_chan((place + chans - 1) % chans, chans)

    barrier = pltpu.get_barrier_semaphore()
    for hop in range(1, ctx):
        pl.semaphore_signal(
            barrier, inc=1, device_id={"ctx": (index + hop) % ctx}, device_id_type=MESH
        )
    for peer in (left, right):
        pl.semaphore_signal(barrier, inc=1, device_id={"chan": peer}, device_id_type=MESH)

    loads = [
        pltpu.make_async_copy(source, target, load_sems.at[k])
        for k, (source, target) in enumerate(
            (
                (taps_in, taps_ref),
                (rate_in, rate_ref),
                (residue_in, residue_ref),
                (skip_in, skip_ref),
                (proj_in, proj_ref),
            )
        )
    ]
    for load in loads:
        load.start()
    if weight_ref.shape[1] == width:
        weight_from = weight_ref
    else:
        weight_from = weight_ref.at[:, pl.ds(pl.multiple_of(chan * width, width), width)]
    weight_copy = pltpu.make_async_copy(weight_from, own_weight, weight_sem)
    weight_copy.start()

    pl.semaphore_wait(barrier, ctx + 1)
    halo_copy = pltpu.make_async_remote_copy(
        src_ref=proj_in.at[:, :, pl.ds(tokens - BLOCK, BLOCK)],
        dst_ref=halo,
        send_sem=halo_sems.at[0],
        recv_sem=halo_sems.at[1],
        device_id={"ctx": (index + 1) % ctx},
        device_id_type=MESH,
    )

    @pl.when(index < ctx - 1)
    def _():
        halo_copy.start()

    loads[0].wait()
    all_groups = taps_ref.shape[1]
    pick = one_hot(
        iota((groups, all_groups), 1) == iota((groups, all_groups), 0) + chan * groups,
        jnp.bfloat16,
    )
    flip = one_hot(
        iota((BLOCK, 2 * BLOCK), 1) == BLOCK - iota((BLOCK, 2 * BLOCK), 0), jnp.bfloat16
    )
    for stream in range(3):
        own = jnp.dot(pick, taps_ref[stream], preferred_element_type=jnp.float32)
        rows = jnp.dot(own.astype(jnp.bfloat16), flip, preferred_element_type=jnp.float32)
        for g in range(groups):
            wide = jnp.broadcast_to(rows[g : g + 1, :], (BLOCK, 2 * BLOCK))
            bands[stream, g] = pltpu.roll(wide, 0, 1, stride=1, stride_axis=0).astype(
                jnp.bfloat16
            )

    for load in loads[1:4]:
        load.wait()
    high = modes * groups
    expand = one_hot(iota((high, modes), 0) // groups == iota((high, modes), 1))
    kept = iota((high, width), 1) // GROUP == iota((high, width), 0) % groups
    spread = one_hot(iota((width, lanes), 0) % GROUP == iota((width, lanes), 1) % GROUP)

    def spread_rows(value):
        tall = lax.dot_general(
            expand,
            value,
            (((1,), (0,)), ((), ())),
            precision=HIGHEST,
            preferred_element_type=jnp.float32,
        )
        return jnp.dot(
            jnp.where(kept, tall, 0.0),
            spread,
            precision=HIGHEST,
            preferred_element_type=jnp.float32,
        )

    rate_s[...] = spread_rows(rate_ref[...])
    residue_s[...] = spread_rows(residue_ref[...]) * jnp.sqrt(2.0 * rate_s[...] / modes)
    skip_rows = jnp.where(
        iota((groups, width), 1) // GROUP == iota((groups, width), 0),
        jnp.broadcast_to(skip_ref[...], (groups, width)),
        0.0,
    )
    skip = jnp.dot(skip_rows, spread, precision=HIGHEST, preferred_element_type=jnp.float32)

    def of_mode(ref, m):
        return ref[m * groups : (m + 1) * groups, :]

    decay = [jnp.exp(-of_mode(rate_s, m)) for m in range(modes)]

    loads[4].wait()

    @pl.when(index > 0)
    def _():
        halo_copy.wait_recv()

    @pl.when(index == 0)
    def _():
        halo[...] = jnp.zeros_like(halo)

    def short(stream, g):
        rows_of = slice(g * GROUP, (g + 1) * GROUP)
        tiles = [proj_ref[stream, rows_of, b * BLOCK : (b + 1) * BLOCK] for b in range(blocks)]
        before = [halo[stream, rows_of, :]] + tiles[:-1]
        signal = jnp.concatenate(
            [jnp.concatenate(before, axis=0), jnp.concatenate(tiles, axis=0)], axis=1
        )
        return lax.dot_general(
            bands[stream, g], signal, (((1,), (1,)), ((), ())), preferred_element_type=jnp.float32
        )

    for g in range(groups):
        mixed[pl.ds(g, BLOCK, stride=groups), :] = short(1, g) * short(2, g)

    def gather_step(r, states):
        x = mixed[pl.ds(pl.multiple_of(r * groups, groups), groups), :]
        return tuple(d * s + x for d, s in zip(decay, states))

    zero = jnp.zeros((groups, lanes), jnp.float32)
    last = lax.fori_loop(0, BLOCK, gather_step, (zero,) * modes, unroll=8)
    at = iota(zero.shape, 1) // GROUP
    for m in range(modes):
        total, hop = last[m], 1
        while hop < blocks:
            moved = jnp.exp(of_mode(rate_s, m) * (-float(BLOCK * hop))) * pltpu.roll(
                total, GROUP * hop, 1
            )
            total = total + jnp.where(at >= hop, moved, 0.0)
            hop *= 2
        state[m * groups : (m + 1) * groups, :] = total

    end_copies = [
        pltpu.make_async_remote_copy(
            src_ref=state,
            dst_ref=ends.at[hop - 1],
            send_sem=end_send.at[hop - 1],
            recv_sem=end_recv.at[hop - 1],
            device_id={"ctx": (index + hop) % ctx},
            device_id_type=MESH,
        )
        for hop in range(1, ctx)
    ]
    for hop in range(1, ctx):

        @pl.when(index < ctx - hop)
        def _():
            end_copies[hop - 1].start()

    for g in range(groups):
        query[pl.ds(g, BLOCK, stride=groups), :] = short(0, g)

    for hop in range(1, ctx):

        @pl.when(index >= hop)
        def _():
            end_copies[hop - 1].wait_recv()

        @pl.when(index < hop)
        def _():
            ends[hop - 1] = jnp.zeros((high, lanes), jnp.float32)

    at_tokens = at.astype(jnp.float32) * float(BLOCK)
    entry, weight = [], []
    for m in range(modes):
        rate = of_mode(rate_s, m)
        per_device = jnp.exp(rate * (-float(tokens)))
        incoming = jnp.zeros_like(zero)
        for hop in range(ctx - 1, 0, -1):
            incoming = per_device * incoming + ends[hop - 1, m * groups : (m + 1) * groups, :]
        incoming = jnp.where(at == blocks - 1, incoming, 0.0)
        hop = 1
        while hop < blocks:
            incoming = incoming + pltpu.roll(incoming, GROUP * hop, 1)
            hop *= 2
        own = jnp.where(at >= 1, pltpu.roll(of_mode(state, m), GROUP, 1), 0.0)
        entry.append(own + jnp.exp(-rate * at_tokens) * incoming)
        weight.append(of_mode(residue_s, m))

    def step(r, states):
        where = pl.ds(pl.multiple_of(r * groups, groups), groups)
        x = mixed[where, :]
        new = tuple(d * s + x for d, s in zip(decay, states))
        parts = [w * s for w, s in zip(weight, new)] + [skip * x]
        while len(parts) > 1:
            parts = [a + b for a, b in zip(parts[::2], parts[1::2])] + (
                [parts[-1]] if len(parts) % 2 else []
            )
        work[where, :] = query[where, :] * parts[0]
        return new

    lax.fori_loop(0, BLOCK, step, tuple(entry), unroll=4)
    per_piece = blocks // PIECES
    for g in range(groups):
        turned = work[pl.ds(g, BLOCK, stride=groups), :].T.astype(jnp.bfloat16)
        for b in range(blocks):
            inside = (b % per_piece) * BLOCK
            gath[
                chan, b // per_piece, g * GROUP : (g + 1) * GROUP, inside : inside + BLOCK
            ] = turned[b * GROUP : (b + 1) * GROUP]

    half = chans // 2

    def ring_copy(way, hop, piece):
        shard = ring_chan((place + chans + (-hop if way == 0 else hop)) % chans, chans)
        return pltpu.make_async_remote_copy(
            src_ref=gath.at[shard, piece],
            dst_ref=gath.at[shard, piece],
            send_sem=ring_send.at[way, hop, piece],
            recv_sem=ring_recv.at[way, hop, piece],
            device_id={"chan": right if way == 0 else left},
            device_id_type=MESH,
        )

    def travels(way, hop, piece):
        if hop < half - 1:
            return True
        return hop == half - 1 and (piece < PIECES // 2) == (way == 0)

    copies = {}
    for piece in range(PIECES):
        for way in range(2):
            copies[way, 0, piece] = ring_copy(way, 0, piece)
            copies[way, 0, piece].start()
    weight_copy.wait()

    def project(shard, piece):
        rows_of = pl.ds(pl.multiple_of(shard * width, width), width)
        return lax.dot_general(
            own_weight[rows_of, :],
            gath[shard, piece],
            (((0,), (0,)), ((), ())),
            preferred_element_type=jnp.float32,
        )

    for piece in range(PIECES):
        acc[piece] = project(chan, piece)
    for hop in range(1, half + 1):
        for piece in range(PIECES):
            arrived = []
            for way in range(2):
                if not travels(way, hop - 1, piece):
                    continue
                copies[way, hop - 1, piece].wait_recv()
                if travels(way, hop, piece):
                    copies[way, hop, piece] = ring_copy(way, hop, piece)
                    copies[way, hop, piece].start()
                arrived.append(
                    ring_chan((place + chans + (-hop if way == 0 else hop)) % chans, chans)
                )
            total = acc[piece]
            for shard in arrived:
                total = total + project(shard, piece)
            if hop == half:
                out_ref[:, piece * cols : (piece + 1) * cols] = total.astype(out_ref.dtype)
            else:
                acc[piece] = total

    for key in copies:
        copies[key].wait_send()

    @pl.when(index < ctx - 1)
    def _():
        halo_copy.wait_send()

    for hop in range(1, ctx):

        @pl.when(index < ctx - hop)
        def _():
            end_copies[hop - 1].wait_send()


def per_device(ctx, chans, proj, taps, rate, residue, skip, out_weight):
    width, tokens = proj.shape[1:]
    modes = rate.shape[1]
    groups, blocks = width // GROUP, tokens // BLOCK
    lanes = blocks * GROUP
    if width % 128:
        out_weight = lax.dynamic_slice_in_dim(
            out_weight, lax.axis_index("chan") * width, width, 1
        )
    vmem = pl.BlockSpec(memory_space=pltpu.VMEM)
    major = pltpu.VMEM((BLOCK * groups, lanes), jnp.float32)
    table = pltpu.VMEM((modes * groups, lanes), jnp.float32)
    return pl.pallas_call(
        functools.partial(fused, ctx, chans),
        out_shape=jax.ShapeDtypeStruct((width, tokens), jnp.bfloat16),
        in_specs=[pl.BlockSpec(memory_space=pltpu.HBM)] * 6,
        out_specs=vmem,
        scratch_shapes=[
            pltpu.VMEM(proj.shape, proj.dtype),
            pltpu.VMEM(taps.shape, taps.dtype),
            pltpu.VMEM((modes, width), jnp.float32),
            pltpu.VMEM((modes, width), jnp.float32),
            pltpu.VMEM((1, width), jnp.float32),
            pltpu.VMEM((3, width, BLOCK), jnp.bfloat16),
            major,
            major,
            major,
            pltpu.VMEM((3, groups, BLOCK, 2 * BLOCK), jnp.bfloat16),
            table,
            table,
            table,
            pltpu.VMEM((ctx - 1, modes * groups, lanes), jnp.float32),
            pltpu.VMEM((chans * width, width), jnp.bfloat16),
            pltpu.VMEM((chans, PIECES, width, tokens // PIECES), jnp.bfloat16),
            pltpu.VMEM((PIECES, width, tokens // PIECES), jnp.float32),
            pltpu.SemaphoreType.DMA,
            pltpu.SemaphoreType.DMA((5,)),
            pltpu.SemaphoreType.DMA((2,)),
            pltpu.SemaphoreType.DMA((ctx - 1,)),
            pltpu.SemaphoreType.DMA((ctx - 1,)),
            pltpu.SemaphoreType.DMA((2, chans // 2, PIECES)),
            pltpu.SemaphoreType.DMA((2, chans // 2, PIECES)),
        ],
        compiler_params=pltpu.CompilerParams(
            vmem_limit_bytes=58 << 20, collective_id=0, has_side_effects=True
        ),
        name="fused",
    )(proj, taps, rate.T, residue.T, skip.reshape(1, width), out_weight)


def solution(mesh):
    in_specs = (P(None, "chan", "ctx"), P(), P("chan", None), P("chan", None), P("chan"), P())
    out_specs = P("chan", "ctx")
    return jax.shard_map(
        functools.partial(per_device, mesh.shape["ctx"], mesh.shape["chan"]),
        mesh=mesh,
        in_specs=in_specs,
        out_specs=out_specs,
        check_vma=False,
    )
```

```python
import functools
import jax
import jax.numpy as jnp
from jax import lax
from jax.experimental import pallas as pl
from jax.experimental.pallas import tpu as pltpu
from jax.sharding import PartitionSpec as P

GROUP = 16
BLOCK = 128
PIECES = 4
MESH = pl.DeviceIdType.MESH
HIGHEST = lax.Precision.HIGHEST


def iota(shape, axis):
    return lax.broadcasted_iota(jnp.int32, shape, axis)


def one_hot(hit, dtype=jnp.float32):
    return hit.astype(jnp.float32).astype(dtype)


def ring_place(chan, n):
    row, side = chan // 2, chan % 2
    return row + side * (n - 1 - 2 * row)


def ring_chan(place, n):
    side = place // (n // 2)
    row = place + side * (n - 1 - 2 * place)
    return 2 * row + side


def fused(
    ctx,
    chans,
    proj_in,
    taps_in,
    rate_in,
    residue_in,
    skip_in,
    weight_ref,
    out_ref,
    proj_ref,
    taps_ref,
    rate_ref,
    residue_ref,
    skip_ref,
    halo,
    query,
    mixed,
    work,
    bands,
    rate_s,
    residue_s,
    state,
    ends,
    own_weight,
    gath,
    acc,
    weight_sem,
    load_sems,
    halo_sems,
    end_send,
    end_recv,
    ring_send,
    ring_recv,
):
    width, tokens = proj_ref.shape[1:]
    modes = rate_ref.shape[0]
    groups, blocks = width // GROUP, tokens // BLOCK
    lanes = blocks * GROUP
    cols = tokens // PIECES
    index = lax.axis_index("ctx")
    chan = lax.axis_index("chan")
    place = ring_place(chan, chans)
    right = ring_chan((place + 1) % chans, chans)
    left = ring_chan((place + chans - 1) % chans, chans)

    barrier = pltpu.get_barrier_semaphore()
    for hop in range(1, ctx):
        pl.semaphore_signal(
            barrier, inc=1, device_id={"ctx": (index + hop) % ctx}, device_id_type=MESH
        )
    for peer in (left, right):
        pl.semaphore_signal(barrier, inc=1, device_id={"chan": peer}, device_id_type=MESH)

    loads = [
        pltpu.make_async_copy(source, target, load_sems.at[k])
        for k, (source, target) in enumerate(
            (
                (taps_in, taps_ref),
                (rate_in, rate_ref),
                (residue_in, residue_ref),
                (skip_in, skip_ref),
                (proj_in, proj_ref),
            )
        )
    ]
    for load in loads:
        load.start()
    if weight_ref.shape[1] == width:
        weight_from = weight_ref
    else:
        weight_from = weight_ref.at[:, pl.ds(pl.multiple_of(chan * width, width), width)]
    weight_copy = pltpu.make_async_copy(weight_from, own_weight, weight_sem)
    weight_copy.start()

    pl.semaphore_wait(barrier, ctx + 1)
    halo_copy = pltpu.make_async_remote_copy(
        src_ref=proj_in.at[:, :, pl.ds(tokens - BLOCK, BLOCK)],
        dst_ref=halo,
        send_sem=halo_sems.at[0],
        recv_sem=halo_sems.at[1],
        device_id={"ctx": (index + 1) % ctx},
        device_id_type=MESH,
    )

    @pl.when(index < ctx - 1)
    def _():
        halo_copy.start()

    loads[0].wait()
    all_groups = taps_ref.shape[1]
    pick = one_hot(
        iota((groups, all_groups), 1) == iota((groups, all_groups), 0) + chan * groups,
        jnp.bfloat16,
    )
    flip = one_hot(
        iota((BLOCK, 2 * BLOCK), 1) == BLOCK - iota((BLOCK, 2 * BLOCK), 0), jnp.bfloat16
    )
    def make_bands(stream):
        own = jnp.dot(pick, taps_ref[stream], preferred_element_type=jnp.float32)
        rows = jnp.dot(own.astype(jnp.bfloat16), flip, preferred_element_type=jnp.float32)
        for g in range(groups):
            wide = jnp.broadcast_to(rows[g : g + 1, :], (BLOCK, 2 * BLOCK))
            bands[stream, g] = pltpu.roll(wide, 0, 1, stride=1, stride_axis=0).astype(
                jnp.bfloat16
            )

    make_bands(1)
    make_bands(2)
    loads[1].wait()
    high = modes * groups
    expand = one_hot(iota((high, modes), 0) // groups == iota((high, modes), 1))
    kept = iota((high, width), 1) // GROUP == iota((high, width), 0) % groups
    spread = one_hot(iota((width, lanes), 0) % GROUP == iota((width, lanes), 1) % GROUP)

    def spread_rows(value):
        tall = lax.dot_general(
            expand,
            value,
            (((1,), (0,)), ((), ())),
            precision=HIGHEST,
            preferred_element_type=jnp.float32,
        )
        return jnp.dot(
            jnp.where(kept, tall, 0.0),
            spread,
            precision=HIGHEST,
            preferred_element_type=jnp.float32,
        )

    rate_s[...] = spread_rows(rate_ref[...])

    def of_mode(ref, m):
        return ref[m * groups : (m + 1) * groups, :]

    decay = [jnp.exp(-of_mode(rate_s, m)) for m in range(modes)]

    loads[4].wait()

    @pl.when(index > 0)
    def _():
        halo_copy.wait_recv()

    @pl.when(index == 0)
    def _():
        halo[...] = jnp.zeros_like(halo)

    def short(stream, g):
        rows_of = slice(g * GROUP, (g + 1) * GROUP)
        tiles = [proj_ref[stream, rows_of, b * BLOCK : (b + 1) * BLOCK] for b in range(blocks)]
        before = [halo[stream, rows_of, :]] + tiles[:-1]
        signal = jnp.concatenate(
            [jnp.concatenate(before, axis=0), jnp.concatenate(tiles, axis=0)], axis=1
        )
        return lax.dot_general(
            bands[stream, g], signal, (((1,), (1,)), ((), ())), preferred_element_type=jnp.float32
        )

    for g in range(groups):
        mixed[pl.ds(g, BLOCK, stride=groups), :] = short(1, g) * short(2, g)

    def gather_step(r, states):
        x = mixed[pl.ds(pl.multiple_of(r * groups, groups), groups), :]
        return tuple(d * s + x for d, s in zip(decay, states))

    zero = jnp.zeros((groups, lanes), jnp.float32)
    last = lax.fori_loop(0, BLOCK, gather_step, (zero,) * modes, unroll=8)
    at = iota(zero.shape, 1) // GROUP
    for m in range(modes):
        total, hop = last[m], 1
        while hop < blocks:
            moved = jnp.exp(of_mode(rate_s, m) * (-float(BLOCK * hop))) * pltpu.roll(
                total, GROUP * hop, 1
            )
            total = total + jnp.where(at >= hop, moved, 0.0)
            hop *= 2
        state[m * groups : (m + 1) * groups, :] = total

    end_copies = [
        pltpu.make_async_remote_copy(
            src_ref=state,
            dst_ref=ends.at[hop - 1],
            send_sem=end_send.at[hop - 1],
            recv_sem=end_recv.at[hop - 1],
            device_id={"ctx": (index + hop) % ctx},
            device_id_type=MESH,
        )
        for hop in range(1, ctx)
    ]
    for hop in range(1, ctx):

        @pl.when(index < ctx - hop)
        def _():
            end_copies[hop - 1].start()

    make_bands(0)
    for g in range(groups):
        query[pl.ds(g, BLOCK, stride=groups), :] = short(0, g)
    loads[2].wait()
    loads[3].wait()
    residue_s[...] = spread_rows(residue_ref[...]) * jnp.sqrt(2.0 * rate_s[...] / modes)
    skip_rows = jnp.where(
        iota((groups, width), 1) // GROUP == iota((groups, width), 0),
        jnp.broadcast_to(skip_ref[...], (groups, width)),
        0.0,
    )
    skip = jnp.dot(skip_rows, spread, precision=HIGHEST, preferred_element_type=jnp.float32)
    at_tokens = at.astype(jnp.float32) * float(BLOCK)
    across = [jnp.exp(of_mode(rate_s, m) * (-float(tokens))) for m in range(modes)]
    shift = [jnp.exp(-of_mode(rate_s, m) * at_tokens) for m in range(modes)]

    for hop in range(1, ctx):

        @pl.when(index >= hop)
        def _():
            end_copies[hop - 1].wait_recv()

        @pl.when(index < hop)
        def _():
            ends[hop - 1] = jnp.zeros((high, lanes), jnp.float32)

    entry, weight = [], []
    for m in range(modes):
        incoming = jnp.zeros_like(zero)
        for hop in range(ctx - 1, 0, -1):
            incoming = across[m] * incoming + ends[hop - 1, m * groups : (m + 1) * groups, :]
        incoming = jnp.where(at == blocks - 1, incoming, 0.0)
        hop = 1
        while hop < blocks:
            incoming = incoming + pltpu.roll(incoming, GROUP * hop, 1)
            hop *= 2
        own = jnp.where(at >= 1, pltpu.roll(of_mode(state, m), GROUP, 1), 0.0)
        entry.append(own + shift[m] * incoming)
        weight.append(of_mode(residue_s, m))

    def step(r, states):
        where = pl.ds(pl.multiple_of(r * groups, groups), groups)
        x = mixed[where, :]
        new = tuple(d * s + x for d, s in zip(decay, states))
        parts = [w * s for w, s in zip(weight, new)] + [skip * x]
        while len(parts) > 1:
            parts = [a + b for a, b in zip(parts[::2], parts[1::2])] + (
                [parts[-1]] if len(parts) % 2 else []
            )
        work[where, :] = query[where, :] * parts[0]
        return new

    lax.fori_loop(0, BLOCK, step, tuple(entry), unroll=4)
    per_piece = blocks // PIECES
    for g in range(groups):
        turned = work[pl.ds(g, BLOCK, stride=groups), :].T.astype(jnp.bfloat16)
        for b in range(blocks):
            inside = (b % per_piece) * BLOCK
            gath[
                chan, b // per_piece, g * GROUP : (g + 1) * GROUP, inside : inside + BLOCK
            ] = turned[b * GROUP : (b + 1) * GROUP]

    half = chans // 2

    def ring_copy(way, hop, piece):
        shard = ring_chan((place + chans + (-hop if way == 0 else hop)) % chans, chans)
        return pltpu.make_async_remote_copy(
            src_ref=gath.at[shard, piece],
            dst_ref=gath.at[shard, piece],
            send_sem=ring_send.at[way, hop, piece],
            recv_sem=ring_recv.at[way, hop, piece],
            device_id={"chan": right if way == 0 else left},
            device_id_type=MESH,
        )

    def travels(way, hop, piece):
        if hop < half - 1:
            return True
        return hop == half - 1 and (piece < PIECES // 2) == (way == 0)

    copies = {}
    for piece in range(PIECES):
        for way in range(2):
            copies[way, 0, piece] = ring_copy(way, 0, piece)
            copies[way, 0, piece].start()
    weight_copy.wait()

    def project(shard, piece):
        rows_of = pl.ds(pl.multiple_of(shard * width, width), width)
        return lax.dot_general(
            own_weight[rows_of, :],
            gath[shard, piece],
            (((0,), (0,)), ((), ())),
            preferred_element_type=jnp.float32,
        )

    for piece in range(PIECES):
        acc[piece] = project(chan, piece)
    for hop in range(1, half + 1):
        for piece in range(PIECES):
            arrived = []
            for way in range(2):
                if not travels(way, hop - 1, piece):
                    continue
                copies[way, hop - 1, piece].wait_recv()
                if travels(way, hop, piece):
                    copies[way, hop, piece] = ring_copy(way, hop, piece)
                    copies[way, hop, piece].start()
                arrived.append(
                    ring_chan((place + chans + (-hop if way == 0 else hop)) % chans, chans)
                )
            total = acc[piece]
            for shard in arrived:
                total = total + project(shard, piece)
            if hop == half:
                out_ref[:, piece * cols : (piece + 1) * cols] = total.astype(out_ref.dtype)
            else:
                acc[piece] = total

    for key in copies:
        copies[key].wait_send()

    @pl.when(index < ctx - 1)
    def _():
        halo_copy.wait_send()

    for hop in range(1, ctx):

        @pl.when(index < ctx - hop)
        def _():
            end_copies[hop - 1].wait_send()


def per_device(ctx, chans, proj, taps, rate, residue, skip, out_weight):
    width, tokens = proj.shape[1:]
    modes = rate.shape[1]
    groups, blocks = width // GROUP, tokens // BLOCK
    lanes = blocks * GROUP
    if width % 128:
        out_weight = lax.dynamic_slice_in_dim(
            out_weight, lax.axis_index("chan") * width, width, 1
        )
    vmem = pl.BlockSpec(memory_space=pltpu.VMEM)
    major = pltpu.VMEM((BLOCK * groups, lanes), jnp.float32)
    table = pltpu.VMEM((modes * groups, lanes), jnp.float32)
    return pl.pallas_call(
        functools.partial(fused, ctx, chans),
        out_shape=jax.ShapeDtypeStruct((width, tokens), jnp.bfloat16),
        in_specs=[pl.BlockSpec(memory_space=pltpu.HBM)] * 6,
        out_specs=vmem,
        scratch_shapes=[
            pltpu.VMEM(proj.shape, proj.dtype),
            pltpu.VMEM(taps.shape, taps.dtype),
            pltpu.VMEM((modes, width), jnp.float32),
            pltpu.VMEM((modes, width), jnp.float32),
            pltpu.VMEM((1, width), jnp.float32),
            pltpu.VMEM((3, width, BLOCK), jnp.bfloat16),
            major,
            major,
            major,
            pltpu.VMEM((3, groups, BLOCK, 2 * BLOCK), jnp.bfloat16),
            table,
            table,
            table,
            pltpu.VMEM((ctx - 1, modes * groups, lanes), jnp.float32),
            pltpu.VMEM((chans * width, width), jnp.bfloat16),
            pltpu.VMEM((chans, PIECES, width, tokens // PIECES), jnp.bfloat16),
            pltpu.VMEM((PIECES, width, tokens // PIECES), jnp.float32),
            pltpu.SemaphoreType.DMA,
            pltpu.SemaphoreType.DMA((5,)),
            pltpu.SemaphoreType.DMA((2,)),
            pltpu.SemaphoreType.DMA((ctx - 1,)),
            pltpu.SemaphoreType.DMA((ctx - 1,)),
            pltpu.SemaphoreType.DMA((2, chans // 2, PIECES)),
            pltpu.SemaphoreType.DMA((2, chans // 2, PIECES)),
        ],
        compiler_params=pltpu.CompilerParams(
            vmem_limit_bytes=58 << 20, collective_id=0, has_side_effects=True
        ),
        name="fused",
    )(proj, taps, rate.T, residue.T, skip.reshape(1, width), out_weight)


def solution(mesh):
    in_specs = (P(None, "chan", "ctx"), P(), P("chan", None), P("chan", None), P("chan"), P())
    out_specs = P("chan", "ctx")
    return jax.shard_map(
        functools.partial(per_device, mesh.shape["ctx"], mesh.shape["chan"]),
        mesh=mesh,
        in_specs=in_specs,
        out_specs=out_specs,
        check_vma=False,
    )
```

```python
import functools
import jax
import jax.numpy as jnp
from jax import lax
from jax.experimental import pallas as pl
from jax.experimental.pallas import tpu as pltpu
from jax.sharding import PartitionSpec as P

GROUP = 16
BLOCK = 128
PIECES = 4
MESH = pl.DeviceIdType.MESH
HIGHEST = lax.Precision.HIGHEST


def iota(shape, axis):
    return lax.broadcasted_iota(jnp.int32, shape, axis)


def one_hot(hit, dtype=jnp.float32):
    return hit.astype(jnp.float32).astype(dtype)


def ring_place(chan, n):
    row, side = chan // 2, chan % 2
    return row + side * (n - 1 - 2 * row)


def ring_chan(place, n):
    side = place // (n // 2)
    row = place + side * (n - 1 - 2 * place)
    return 2 * row + side


def fused(
    ctx,
    chans,
    proj_in,
    taps_in,
    rate_in,
    residue_in,
    skip_in,
    weight_ref,
    out_ref,
    proj_ref,
    taps_ref,
    rate_ref,
    residue_ref,
    skip_ref,
    halo,
    query,
    mixed,
    work,
    bands,
    rate_s,
    residue_s,
    state,
    ends,
    own_weight,
    gath,
    acc,
    weight_sem,
    load_sems,
    halo_sems,
    end_send,
    end_recv,
    ring_send,
    ring_recv,
):
    width, tokens = proj_ref.shape[1:]
    modes = rate_ref.shape[0]
    groups, blocks = width // GROUP, tokens // BLOCK
    lanes = blocks * GROUP
    cols = tokens // PIECES
    index = lax.axis_index("ctx")
    chan = lax.axis_index("chan")
    place = ring_place(chan, chans)
    right = ring_chan((place + 1) % chans, chans)
    left = ring_chan((place + chans - 1) % chans, chans)

    barrier = pltpu.get_barrier_semaphore()
    for hop in range(1, ctx):
        pl.semaphore_signal(
            barrier, inc=1, device_id={"ctx": (index + hop) % ctx}, device_id_type=MESH
        )
    for peer in (left, right):
        pl.semaphore_signal(barrier, inc=1, device_id={"chan": peer}, device_id_type=MESH)

    loads = [
        pltpu.make_async_copy(source, target, load_sems.at[k])
        for k, (source, target) in enumerate(
            (
                (taps_in, taps_ref),
                (rate_in, rate_ref),
                (residue_in, residue_ref),
                (skip_in, skip_ref),
                (proj_in, proj_ref),
            )
        )
    ]
    for load in loads:
        load.start()
    if weight_ref.shape[1] == width:
        weight_from = weight_ref
    else:
        weight_from = weight_ref.at[:, pl.ds(pl.multiple_of(chan * width, width), width)]
    weight_copy = pltpu.make_async_copy(weight_from, own_weight, weight_sem)
    weight_copy.start()

    pl.semaphore_wait(barrier, ctx + 1)
    halo_copy = pltpu.make_async_remote_copy(
        src_ref=proj_in.at[:, :, pl.ds(tokens - BLOCK, BLOCK)],
        dst_ref=halo,
        send_sem=halo_sems.at[0],
        recv_sem=halo_sems.at[1],
        device_id={"ctx": (index + 1) % ctx},
        device_id_type=MESH,
    )

    @pl.when(index < ctx - 1)
    def _():
        halo_copy.start()

    loads[0].wait()
    all_groups = taps_ref.shape[1]
    pick = one_hot(
        iota((groups, all_groups), 1) == iota((groups, all_groups), 0) + chan * groups,
        jnp.bfloat16,
    )
    flip = one_hot(
        iota((BLOCK, 2 * BLOCK), 1) == BLOCK - iota((BLOCK, 2 * BLOCK), 0), jnp.bfloat16
    )
    def make_bands(stream):
        own = jnp.dot(pick, taps_ref[stream], preferred_element_type=jnp.float32)
        rows = jnp.dot(own.astype(jnp.bfloat16), flip, preferred_element_type=jnp.float32)
        for g in range(groups):
            wide = jnp.broadcast_to(rows[g : g + 1, :], (BLOCK, 2 * BLOCK))
            bands[stream, g] = pltpu.roll(wide, 0, 1, stride=1, stride_axis=0).astype(
                jnp.bfloat16
            )

    make_bands(1)
    make_bands(2)
    loads[1].wait()
    high = modes * groups
    expand = one_hot(iota((high, modes), 0) // groups == iota((high, modes), 1))
    kept = iota((high, width), 1) // GROUP == iota((high, width), 0) % groups
    spread = one_hot(iota((width, lanes), 0) % GROUP == iota((width, lanes), 1) % GROUP)

    def spread_rows(value):
        tall = lax.dot_general(
            expand,
            value,
            (((1,), (0,)), ((), ())),
            precision=HIGHEST,
            preferred_element_type=jnp.float32,
        )
        return jnp.dot(
            jnp.where(kept, tall, 0.0),
            spread,
            precision=HIGHEST,
            preferred_element_type=jnp.float32,
        )

    rate_s[...] = spread_rows(rate_ref[...])

    def of_mode(ref, m):
        return ref[m * groups : (m + 1) * groups, :]

    decay = [jnp.exp(-of_mode(rate_s, m)) for m in range(modes)]

    loads[4].wait()

    @pl.when(index > 0)
    def _():
        halo_copy.wait_recv()

    @pl.when(index == 0)
    def _():
        halo[...] = jnp.zeros_like(halo)

    def short(stream, g):
        rows_of = slice(g * GROUP, (g + 1) * GROUP)
        tiles = [proj_ref[stream, rows_of, b * BLOCK : (b + 1) * BLOCK] for b in range(blocks)]
        before = [halo[stream, rows_of, :]] + tiles[:-1]
        signal = jnp.concatenate(
            [jnp.concatenate(before, axis=0), jnp.concatenate(tiles, axis=0)], axis=1
        )
        return lax.dot_general(
            bands[stream, g], signal, (((1,), (1,)), ((), ())), preferred_element_type=jnp.float32
        )

    for g in range(groups):
        mixed[pl.ds(g, BLOCK, stride=groups), :] = short(1, g) * short(2, g)

    def gather_step(r, states):
        x = mixed[pl.ds(pl.multiple_of(r * groups, groups), groups), :]
        return tuple(d * s + x for d, s in zip(decay, states))

    zero = jnp.zeros((groups, lanes), jnp.float32)
    last = lax.fori_loop(0, BLOCK, gather_step, (zero,) * modes, unroll=8)
    at = iota(zero.shape, 1) // GROUP
    for m in range(modes):
        total, hop = last[m], 1
        while hop < blocks:
            moved = jnp.exp(of_mode(rate_s, m) * (-float(BLOCK * hop))) * pltpu.roll(
                total, GROUP * hop, 1
            )
            total = total + jnp.where(at >= hop, moved, 0.0)
            hop *= 2
        state[m * groups : (m + 1) * groups, :] = total

    end_copies = [
        pltpu.make_async_remote_copy(
            src_ref=state,
            dst_ref=ends.at[hop - 1],
            send_sem=end_send.at[hop - 1],
            recv_sem=end_recv.at[hop - 1],
            device_id={"ctx": (index + hop) % ctx},
            device_id_type=MESH,
        )
        for hop in range(1, ctx)
    ]
    for hop in range(1, ctx):

        @pl.when(index < ctx - hop)
        def _():
            end_copies[hop - 1].start()

    make_bands(0)
    for g in range(groups):
        query[pl.ds(g, BLOCK, stride=groups), :] = short(0, g)
    loads[2].wait()
    loads[3].wait()
    residue_s[...] = spread_rows(residue_ref[...]) * jnp.sqrt(2.0 * rate_s[...] / modes)
    skip_rows = jnp.where(
        iota((groups, width), 1) // GROUP == iota((groups, width), 0),
        jnp.broadcast_to(skip_ref[...], (groups, width)),
        0.0,
    )
    skip = jnp.dot(skip_rows, spread, precision=HIGHEST, preferred_element_type=jnp.float32)
    at_tokens = at.astype(jnp.float32) * float(BLOCK)
    across = [jnp.exp(of_mode(rate_s, m) * (-float(tokens))) for m in range(modes)]
    shift = [jnp.exp(-of_mode(rate_s, m) * at_tokens) for m in range(modes)]

    for hop in range(1, ctx):

        @pl.when(index >= hop)
        def _():
            end_copies[hop - 1].wait_recv()

        @pl.when(index < hop)
        def _():
            ends[hop - 1] = jnp.zeros((high, lanes), jnp.float32)

    entry, weight = [], []
    for m in range(modes):
        incoming = jnp.zeros_like(zero)
        for hop in range(ctx - 1, 0, -1):
            incoming = across[m] * incoming + ends[hop - 1, m * groups : (m + 1) * groups, :]
        incoming = jnp.where(at == blocks - 1, incoming, 0.0)
        hop = 1
        while hop < blocks:
            incoming = incoming + pltpu.roll(incoming, GROUP * hop, 1)
            hop *= 2
        own = jnp.where(at >= 1, pltpu.roll(of_mode(state, m), GROUP, 1), 0.0)
        entry.append(own + shift[m] * incoming)
        weight.append(of_mode(residue_s, m))

    def step(r, states):
        where = pl.ds(pl.multiple_of(r * groups, groups), groups)
        x = mixed[where, :]
        new = tuple(d * s + x for d, s in zip(decay, states))
        parts = [w * s for w, s in zip(weight, new)] + [skip * x]
        while len(parts) > 1:
            parts = [a + b for a, b in zip(parts[::2], parts[1::2])] + (
                [parts[-1]] if len(parts) % 2 else []
            )
        work[where, :] = query[where, :] * parts[0]
        return new

    lax.fori_loop(0, BLOCK, step, tuple(entry), unroll=4)
    per_piece = blocks // PIECES
    for g in range(groups):
        turned = work[pl.ds(g, BLOCK, stride=groups), :].T.astype(jnp.bfloat16)
        for b in range(blocks):
            inside = (b % per_piece) * BLOCK
            gath[
                chan, b // per_piece, g * GROUP : (g + 1) * GROUP, inside : inside + BLOCK
            ] = turned[b * GROUP : (b + 1) * GROUP]

    half = chans // 2

    def ring_copy(way, hop, piece):
        shard = ring_chan((place + chans + (-hop if way == 0 else hop)) % chans, chans)
        return pltpu.make_async_remote_copy(
            src_ref=gath.at[shard, piece],
            dst_ref=gath.at[shard, piece],
            send_sem=ring_send.at[way, hop, piece],
            recv_sem=ring_recv.at[way, hop, piece],
            device_id={"chan": right if way == 0 else left},
            device_id_type=MESH,
        )

    def travels(way, hop, piece):
        if hop < half - 1:
            return True
        return hop == half - 1 and (piece < PIECES // 2) == (way == 0)

    copies = {}
    for piece in range(PIECES):
        for way in range(2):
            copies[way, 0, piece] = ring_copy(way, 0, piece)
            copies[way, 0, piece].start()
    weight_copy.wait()

    def project(shard, piece):
        rows_of = pl.ds(pl.multiple_of(shard * width, width), width)
        return lax.dot_general(
            own_weight[rows_of, :],
            gath[shard, piece],
            (((0,), (0,)), ((), ())),
            preferred_element_type=jnp.float32,
        )

    for piece in range(PIECES):
        acc[piece] = project(chan, piece)
    for hop in range(1, half + 1):
        for piece in range(PIECES):
            arrived = []
            for way in range(2):
                if not travels(way, hop - 1, piece):
                    continue
                copies[way, hop - 1, piece].wait_recv()
                if travels(way, hop, piece):
                    copies[way, hop, piece] = ring_copy(way, hop, piece)
                    copies[way, hop, piece].start()
                arrived.append(
                    ring_chan((place + chans + (-hop if way == 0 else hop)) % chans, chans)
                )
            total = acc[piece]
            for shard in arrived:
                total = total + project(shard, piece)
            if hop == half:
                out_ref[:, piece * cols : (piece + 1) * cols] = total.astype(out_ref.dtype)
            else:
                acc[piece] = total

    for key in copies:
        copies[key].wait_send()

    @pl.when(index < ctx - 1)
    def _():
        halo_copy.wait_send()

    for hop in range(1, ctx):

        @pl.when(index < ctx - hop)
        def _():
            end_copies[hop - 1].wait_send()


def per_device(ctx, chans, proj, taps, rate, residue, skip, out_weight):
    width, tokens = proj.shape[1:]
    modes = rate.shape[1]
    groups, blocks = width // GROUP, tokens // BLOCK
    lanes = blocks * GROUP
    if width % 128:
        out_weight = lax.dynamic_slice_in_dim(
            out_weight, lax.axis_index("chan") * width, width, 1
        )
    vmem = pl.BlockSpec(memory_space=pltpu.VMEM)
    major = pltpu.VMEM((BLOCK * groups, lanes), jnp.float32)
    table = pltpu.VMEM((modes * groups, lanes), jnp.float32)
    return pl.pallas_call(
        functools.partial(fused, ctx, chans),
        out_shape=pltpu.VMEM((width, tokens), jnp.bfloat16),
        in_specs=[pl.BlockSpec(memory_space=pltpu.HBM)] * 6,
        out_specs=vmem,
        scratch_shapes=[
            pltpu.VMEM(proj.shape, proj.dtype),
            pltpu.VMEM(taps.shape, taps.dtype),
            pltpu.VMEM((modes, width), jnp.float32),
            pltpu.VMEM((modes, width), jnp.float32),
            pltpu.VMEM((1, width), jnp.float32),
            pltpu.VMEM((3, width, BLOCK), jnp.bfloat16),
            major,
            major,
            major,
            pltpu.VMEM((3, groups, BLOCK, 2 * BLOCK), jnp.bfloat16),
            table,
            table,
            table,
            pltpu.VMEM((ctx - 1, modes * groups, lanes), jnp.float32),
            pltpu.VMEM((chans * width, width), jnp.bfloat16),
            pltpu.VMEM((chans, PIECES, width, tokens // PIECES), jnp.bfloat16),
            pltpu.VMEM((PIECES, width, tokens // PIECES), jnp.float32),
            pltpu.SemaphoreType.DMA,
            pltpu.SemaphoreType.DMA((5,)),
            pltpu.SemaphoreType.DMA((2,)),
            pltpu.SemaphoreType.DMA((ctx - 1,)),
            pltpu.SemaphoreType.DMA((ctx - 1,)),
            pltpu.SemaphoreType.DMA((2, chans // 2, PIECES)),
            pltpu.SemaphoreType.DMA((2, chans // 2, PIECES)),
        ],
        compiler_params=pltpu.CompilerParams(
            vmem_limit_bytes=58 << 20, collective_id=0, has_side_effects=True
        ),
        name="fused",
    )(proj, taps, rate.T, residue.T, skip.reshape(1, width), out_weight)


def solution(mesh):
    in_specs = (P(None, "chan", "ctx"), P(), P("chan", None), P("chan", None), P("chan"), P())
    out_specs = P("chan", "ctx")
    return jax.shard_map(
        functools.partial(per_device, mesh.shape["ctx"], mesh.shape["chan"]),
        mesh=mesh,
        in_specs=in_specs,
        out_specs=out_specs,
        check_vma=False,
    )
```

```python
import functools
import jax
import jax.numpy as jnp
from jax import lax
from jax.experimental import pallas as pl
from jax.experimental.pallas import tpu as pltpu
from jax.sharding import PartitionSpec as P

GROUP = 16
BLOCK = 128
PIECES = 8
MESH = pl.DeviceIdType.MESH
HIGHEST = lax.Precision.HIGHEST


def iota(shape, axis):
    return lax.broadcasted_iota(jnp.int32, shape, axis)


def one_hot(hit, dtype=jnp.float32):
    return hit.astype(jnp.float32).astype(dtype)


def ring_place(chan, n):
    row, side = chan // 2, chan % 2
    return row + side * (n - 1 - 2 * row)


def ring_chan(place, n):
    side = place // (n // 2)
    row = place + side * (n - 1 - 2 * place)
    return 2 * row + side


def fused(
    ctx,
    chans,
    proj_in,
    taps_in,
    rate_in,
    residue_in,
    skip_in,
    weight_ref,
    out_ref,
    proj_ref,
    taps_ref,
    rate_ref,
    residue_ref,
    skip_ref,
    halo,
    query,
    mixed,
    work,
    bands,
    rate_s,
    residue_s,
    state,
    ends,
    own_weight,
    gath,
    acc,
    weight_sem,
    load_sems,
    halo_sems,
    end_send,
    end_recv,
    ring_send,
    ring_recv,
):
    width, tokens = proj_ref.shape[1:]
    modes = rate_ref.shape[0]
    groups, blocks = width // GROUP, tokens // BLOCK
    lanes = blocks * GROUP
    cols = tokens // PIECES
    index = lax.axis_index("ctx")
    chan = lax.axis_index("chan")
    place = ring_place(chan, chans)
    right = ring_chan((place + 1) % chans, chans)
    left = ring_chan((place + chans - 1) % chans, chans)

    barrier = pltpu.get_barrier_semaphore()
    for hop in range(1, ctx):
        pl.semaphore_signal(
            barrier, inc=1, device_id={"ctx": (index + hop) % ctx}, device_id_type=MESH
        )
    for peer in (left, right):
        pl.semaphore_signal(barrier, inc=1, device_id={"chan": peer}, device_id_type=MESH)

    loads = [
        pltpu.make_async_copy(source, target, load_sems.at[k])
        for k, (source, target) in enumerate(
            (
                (taps_in, taps_ref),
                (rate_in, rate_ref),
                (residue_in, residue_ref),
                (skip_in, skip_ref),
                (proj_in, proj_ref),
            )
        )
    ]
    for load in loads:
        load.start()
    if weight_ref.shape[1] == width:
        weight_from = weight_ref
    else:
        weight_from = weight_ref.at[:, pl.ds(pl.multiple_of(chan * width, width), width)]
    weight_copy = pltpu.make_async_copy(weight_from, own_weight, weight_sem)
    weight_copy.start()

    pl.semaphore_wait(barrier, ctx + 1)
    halo_copy = pltpu.make_async_remote_copy(
        src_ref=proj_in.at[:, :, pl.ds(tokens - BLOCK, BLOCK)],
        dst_ref=halo,
        send_sem=halo_sems.at[0],
        recv_sem=halo_sems.at[1],
        device_id={"ctx": (index + 1) % ctx},
        device_id_type=MESH,
    )

    @pl.when(index < ctx - 1)
    def _():
        halo_copy.start()

    loads[0].wait()
    all_groups = taps_ref.shape[1]
    pick = one_hot(
        iota((groups, all_groups), 1) == iota((groups, all_groups), 0) + chan * groups,
        jnp.bfloat16,
    )
    flip = one_hot(
        iota((BLOCK, 2 * BLOCK), 1) == BLOCK - iota((BLOCK, 2 * BLOCK), 0), jnp.bfloat16
    )
    def make_bands(stream):
        own = jnp.dot(pick, taps_ref[stream], preferred_element_type=jnp.float32)
        rows = jnp.dot(own.astype(jnp.bfloat16), flip, preferred_element_type=jnp.float32)
        for g in range(groups):
            wide = jnp.broadcast_to(rows[g : g + 1, :], (BLOCK, 2 * BLOCK))
            bands[stream, g] = pltpu.roll(wide, 0, 1, stride=1, stride_axis=0).astype(
                jnp.bfloat16
            )

    make_bands(1)
    make_bands(2)
    loads[1].wait()
    high = modes * groups
    expand = one_hot(iota((high, modes), 0) // groups == iota((high, modes), 1))
    kept = iota((high, width), 1) // GROUP == iota((high, width), 0) % groups
    spread = one_hot(iota((width, lanes), 0) % GROUP == iota((width, lanes), 1) % GROUP)

    def spread_rows(value):
        tall = lax.dot_general(
            expand,
            value,
            (((1,), (0,)), ((), ())),
            precision=HIGHEST,
            preferred_element_type=jnp.float32,
        )
        return jnp.dot(
            jnp.where(kept, tall, 0.0),
            spread,
            precision=HIGHEST,
            preferred_element_type=jnp.float32,
        )

    rate_s[...] = spread_rows(rate_ref[...])

    def of_mode(ref, m):
        return ref[m * groups : (m + 1) * groups, :]

    decay = [jnp.exp(-of_mode(rate_s, m)) for m in range(modes)]

    loads[4].wait()

    @pl.when(index > 0)
    def _():
        halo_copy.wait_recv()

    @pl.when(index == 0)
    def _():
        halo[...] = jnp.zeros_like(halo)

    def short(stream, g):
        rows_of = slice(g * GROUP, (g + 1) * GROUP)
        tiles = [proj_ref[stream, rows_of, b * BLOCK : (b + 1) * BLOCK] for b in range(blocks)]
        before = [halo[stream, rows_of, :]] + tiles[:-1]
        signal = jnp.concatenate(
            [jnp.concatenate(before, axis=0), jnp.concatenate(tiles, axis=0)], axis=1
        )
        return lax.dot_general(
            bands[stream, g], signal, (((1,), (1,)), ((), ())), preferred_element_type=jnp.float32
        )

    for g in range(groups):
        mixed[pl.ds(g, BLOCK, stride=groups), :] = short(1, g) * short(2, g)

    def gather_step(r, states):
        x = mixed[pl.ds(pl.multiple_of(r * groups, groups), groups), :]
        return tuple(d * s + x for d, s in zip(decay, states))

    zero = jnp.zeros((groups, lanes), jnp.float32)
    last = lax.fori_loop(0, BLOCK, gather_step, (zero,) * modes, unroll=8)
    at = iota(zero.shape, 1) // GROUP
    for m in range(modes):
        total, hop = last[m], 1
        while hop < blocks:
            moved = jnp.exp(of_mode(rate_s, m) * (-float(BLOCK * hop))) * pltpu.roll(
                total, GROUP * hop, 1
            )
            total = total + jnp.where(at >= hop, moved, 0.0)
            hop *= 2
        state[m * groups : (m + 1) * groups, :] = total

    end_copies = [
        pltpu.make_async_remote_copy(
            src_ref=state,
            dst_ref=ends.at[hop - 1],
            send_sem=end_send.at[hop - 1],
            recv_sem=end_recv.at[hop - 1],
            device_id={"ctx": (index + hop) % ctx},
            device_id_type=MESH,
        )
        for hop in range(1, ctx)
    ]
    for hop in range(1, ctx):

        @pl.when(index < ctx - hop)
        def _():
            end_copies[hop - 1].start()

    make_bands(0)
    for g in range(groups):
        query[pl.ds(g, BLOCK, stride=groups), :] = short(0, g)
    loads[2].wait()
    loads[3].wait()
    residue_s[...] = spread_rows(residue_ref[...]) * jnp.sqrt(2.0 * rate_s[...] / modes)
    skip_rows = jnp.where(
        iota((groups, width), 1) // GROUP == iota((groups, width), 0),
        jnp.broadcast_to(skip_ref[...], (groups, width)),
        0.0,
    )
    skip = jnp.dot(skip_rows, spread, precision=HIGHEST, preferred_element_type=jnp.float32)
    at_tokens = at.astype(jnp.float32) * float(BLOCK)
    across = [jnp.exp(of_mode(rate_s, m) * (-float(tokens))) for m in range(modes)]
    shift = [jnp.exp(-of_mode(rate_s, m) * at_tokens) for m in range(modes)]

    for hop in range(1, ctx):

        @pl.when(index >= hop)
        def _():
            end_copies[hop - 1].wait_recv()

        @pl.when(index < hop)
        def _():
            ends[hop - 1] = jnp.zeros((high, lanes), jnp.float32)

    entry, weight = [], []
    for m in range(modes):
        incoming = jnp.zeros_like(zero)
        for hop in range(ctx - 1, 0, -1):
            incoming = across[m] * incoming + ends[hop - 1, m * groups : (m + 1) * groups, :]
        incoming = jnp.where(at == blocks - 1, incoming, 0.0)
        hop = 1
        while hop < blocks:
            incoming = incoming + pltpu.roll(incoming, GROUP * hop, 1)
            hop *= 2
        own = jnp.where(at >= 1, pltpu.roll(of_mode(state, m), GROUP, 1), 0.0)
        entry.append(own + shift[m] * incoming)
        weight.append(of_mode(residue_s, m))

    def step(r, states):
        where = pl.ds(pl.multiple_of(r * groups, groups), groups)
        x = mixed[where, :]
        new = tuple(d * s + x for d, s in zip(decay, states))
        parts = [w * s for w, s in zip(weight, new)] + [skip * x]
        while len(parts) > 1:
            parts = [a + b for a, b in zip(parts[::2], parts[1::2])] + (
                [parts[-1]] if len(parts) % 2 else []
            )
        work[where, :] = query[where, :] * parts[0]
        return new

    lax.fori_loop(0, BLOCK, step, tuple(entry), unroll=4)
    per_piece = blocks // PIECES
    for g in range(groups):
        turned = work[pl.ds(g, BLOCK, stride=groups), :].T.astype(jnp.bfloat16)
        for b in range(blocks):
            inside = (b % per_piece) * BLOCK
            gath[
                chan, b // per_piece, g * GROUP : (g + 1) * GROUP, inside : inside + BLOCK
            ] = turned[b * GROUP : (b + 1) * GROUP]

    half = chans // 2

    def ring_copy(way, hop, piece):
        shard = ring_chan((place + chans + (-hop if way == 0 else hop)) % chans, chans)
        return pltpu.make_async_remote_copy(
            src_ref=gath.at[shard, piece],
            dst_ref=gath.at[shard, piece],
            send_sem=ring_send.at[way, hop, piece],
            recv_sem=ring_recv.at[way, hop, piece],
            device_id={"chan": right if way == 0 else left},
            device_id_type=MESH,
        )

    def travels(way, hop, piece):
        if hop < half - 1:
            return True
        return hop == half - 1 and (piece < PIECES // 2) == (way == 0)

    copies = {}
    for piece in range(PIECES):
        for way in range(2):
            copies[way, 0, piece] = ring_copy(way, 0, piece)
            copies[way, 0, piece].start()
    weight_copy.wait()

    def project(shard, piece):
        rows_of = pl.ds(pl.multiple_of(shard * width, width), width)
        return lax.dot_general(
            own_weight[rows_of, :],
            gath[shard, piece],
            (((0,), (0,)), ((), ())),
            preferred_element_type=jnp.float32,
        )

    for piece in range(PIECES):
        acc[piece] = project(chan, piece)
    for hop in range(1, half + 1):
        for piece in range(PIECES):
            arrived = []
            for way in range(2):
                if not travels(way, hop - 1, piece):
                    continue
                copies[way, hop - 1, piece].wait_recv()
                if travels(way, hop, piece):
                    copies[way, hop, piece] = ring_copy(way, hop, piece)
                    copies[way, hop, piece].start()
                arrived.append(
                    ring_chan((place + chans + (-hop if way == 0 else hop)) % chans, chans)
                )
            total = acc[piece]
            for shard in arrived:
                total = total + project(shard, piece)
            if hop == half:
                out_ref[:, piece * cols : (piece + 1) * cols] = total.astype(out_ref.dtype)
            else:
                acc[piece] = total

    for key in copies:
        copies[key].wait_send()

    @pl.when(index < ctx - 1)
    def _():
        halo_copy.wait_send()

    for hop in range(1, ctx):

        @pl.when(index < ctx - hop)
        def _():
            end_copies[hop - 1].wait_send()


def per_device(ctx, chans, proj, taps, rate, residue, skip, out_weight):
    width, tokens = proj.shape[1:]
    modes = rate.shape[1]
    groups, blocks = width // GROUP, tokens // BLOCK
    lanes = blocks * GROUP
    if width % 128:
        out_weight = lax.dynamic_slice_in_dim(
            out_weight, lax.axis_index("chan") * width, width, 1
        )
    vmem = pl.BlockSpec(memory_space=pltpu.VMEM)
    major = pltpu.VMEM((BLOCK * groups, lanes), jnp.float32)
    table = pltpu.VMEM((modes * groups, lanes), jnp.float32)
    return pl.pallas_call(
        functools.partial(fused, ctx, chans),
        out_shape=pltpu.VMEM((width, tokens), jnp.bfloat16),
        in_specs=[pl.BlockSpec(memory_space=pltpu.HBM)] * 6,
        out_specs=vmem,
        scratch_shapes=[
            pltpu.VMEM(proj.shape, proj.dtype),
            pltpu.VMEM(taps.shape, taps.dtype),
            pltpu.VMEM((modes, width), jnp.float32),
            pltpu.VMEM((modes, width), jnp.float32),
            pltpu.VMEM((1, width), jnp.float32),
            pltpu.VMEM((3, width, BLOCK), jnp.bfloat16),
            major,
            major,
            major,
            pltpu.VMEM((3, groups, BLOCK, 2 * BLOCK), jnp.bfloat16),
            table,
            table,
            table,
            pltpu.VMEM((ctx - 1, modes * groups, lanes), jnp.float32),
            pltpu.VMEM((chans * width, width), jnp.bfloat16),
            pltpu.VMEM((chans, PIECES, width, tokens // PIECES), jnp.bfloat16),
            pltpu.VMEM((PIECES, width, tokens // PIECES), jnp.float32),
            pltpu.SemaphoreType.DMA,
            pltpu.SemaphoreType.DMA((5,)),
            pltpu.SemaphoreType.DMA((2,)),
            pltpu.SemaphoreType.DMA((ctx - 1,)),
            pltpu.SemaphoreType.DMA((ctx - 1,)),
            pltpu.SemaphoreType.DMA((2, chans // 2, PIECES)),
            pltpu.SemaphoreType.DMA((2, chans // 2, PIECES)),
        ],
        compiler_params=pltpu.CompilerParams(
            vmem_limit_bytes=58 << 20, collective_id=0, has_side_effects=True
        ),
        name="fused",
    )(proj, taps, rate.T, residue.T, skip.reshape(1, width), out_weight)


def solution(mesh):
    in_specs = (P(None, "chan", "ctx"), P(), P("chan", None), P("chan", None), P("chan"), P())
    out_specs = P("chan", "ctx")
    return jax.shard_map(
        functools.partial(per_device, mesh.shape["ctx"], mesh.shape["chan"]),
        mesh=mesh,
        in_specs=in_specs,
        out_specs=out_specs,
        check_vma=False,
    )
```

```python
import functools
import jax
import jax.numpy as jnp
from jax import lax
from jax.experimental import pallas as pl
from jax.experimental.pallas import tpu as pltpu
from jax.sharding import PartitionSpec as P

GROUP = 16
BLOCK = 128
PIECES = 4
MESH = pl.DeviceIdType.MESH
HIGHEST = lax.Precision.HIGHEST


def iota(shape, axis):
    return lax.broadcasted_iota(jnp.int32, shape, axis)


def one_hot(hit, dtype=jnp.float32):
    return hit.astype(jnp.float32).astype(dtype)


def ring_place(chan, n):
    row, side = chan // 2, chan % 2
    return row + side * (n - 1 - 2 * row)


def ring_chan(place, n):
    side = place // (n // 2)
    row = place + side * (n - 1 - 2 * place)
    return 2 * row + side


def fused(
    ctx,
    chans,
    proj_in,
    taps_in,
    rate_in,
    residue_in,
    skip_in,
    weight_ref,
    out_ref,
    proj_ref,
    taps_ref,
    rate_ref,
    residue_ref,
    skip_ref,
    halo,
    query,
    mixed,
    work,
    bands,
    rate_s,
    residue_s,
    state,
    ends,
    own_weight,
    gath,
    acc,
    weight_sem,
    load_sems,
    halo_sems,
    end_send,
    end_recv,
    ring_send,
    ring_recv,
):
    width, tokens = proj_ref.shape[1:]
    modes = rate_ref.shape[0]
    groups, blocks = width // GROUP, tokens // BLOCK
    lanes = blocks * GROUP
    cols = tokens // PIECES
    index = lax.axis_index("ctx")
    chan = lax.axis_index("chan")
    place = ring_place(chan, chans)
    right = ring_chan((place + 1) % chans, chans)
    left = ring_chan((place + chans - 1) % chans, chans)

    barrier = pltpu.get_barrier_semaphore()
    for hop in range(1, ctx):
        pl.semaphore_signal(
            barrier, inc=1, device_id={"ctx": (index + hop) % ctx}, device_id_type=MESH
        )
    for peer in (left, right):
        pl.semaphore_signal(barrier, inc=1, device_id={"chan": peer}, device_id_type=MESH)

    loads = [
        pltpu.make_async_copy(source, target, load_sems.at[k])
        for k, (source, target) in enumerate(
            (
                (taps_in, taps_ref),
                (rate_in, rate_ref),
                (residue_in, residue_ref),
                (skip_in, skip_ref),
                (proj_in, proj_ref),
            )
        )
    ]
    for load in loads:
        load.start()
    if weight_ref.shape[1] == width:
        weight_from = weight_ref
    else:
        weight_from = weight_ref.at[:, pl.ds(pl.multiple_of(chan * width, width), width)]
    weight_copy = pltpu.make_async_copy(weight_from, own_weight, weight_sem)
    weight_copy.start()

    pl.semaphore_wait(barrier, ctx + 1)
    halo_copy = pltpu.make_async_remote_copy(
        src_ref=proj_in.at[:, :, pl.ds(tokens - BLOCK, BLOCK)],
        dst_ref=halo,
        send_sem=halo_sems.at[0],
        recv_sem=halo_sems.at[1],
        device_id={"ctx": (index + 1) % ctx},
        device_id_type=MESH,
    )

    @pl.when(index < ctx - 1)
    def _():
        halo_copy.start()

    loads[0].wait()
    all_groups = taps_ref.shape[1]
    pick = one_hot(
        iota((groups, all_groups), 1) == iota((groups, all_groups), 0) + chan * groups,
        jnp.bfloat16,
    )
    flip = one_hot(
        iota((BLOCK, 2 * BLOCK), 1) == BLOCK - iota((BLOCK, 2 * BLOCK), 0), jnp.bfloat16
    )
    def make_bands(stream):
        own = jnp.dot(pick, taps_ref[stream], preferred_element_type=jnp.float32)
        rows = jnp.dot(own.astype(jnp.bfloat16), flip, preferred_element_type=jnp.float32)
        for g in range(groups):
            wide = jnp.broadcast_to(rows[g : g + 1, :], (BLOCK, 2 * BLOCK))
            bands[stream, g] = pltpu.roll(wide, 0, 1, stride=1, stride_axis=0).astype(
                jnp.bfloat16
            )

    make_bands(1)
    make_bands(2)
    loads[1].wait()
    high = modes * groups
    expand = one_hot(iota((high, modes), 0) // groups == iota((high, modes), 1))
    kept = iota((high, width), 1) // GROUP == iota((high, width), 0) % groups
    spread = one_hot(iota((width, lanes), 0) % GROUP == iota((width, lanes), 1) % GROUP)

    def spread_rows(value):
        tall = lax.dot_general(
            expand,
            value,
            (((1,), (0,)), ((), ())),
            precision=HIGHEST,
            preferred_element_type=jnp.float32,
        )
        return jnp.dot(
            jnp.where(kept, tall, 0.0),
            spread,
            precision=HIGHEST,
            preferred_element_type=jnp.float32,
        )

    rate_s[...] = spread_rows(rate_ref[...])

    def of_mode(ref, m):
        return ref[m * groups : (m + 1) * groups, :]

    decay = [jnp.exp(-of_mode(rate_s, m)) for m in range(modes)]

    loads[4].wait()

    @pl.when(index > 0)
    def _():
        halo_copy.wait_recv()

    @pl.when(index == 0)
    def _():
        halo[...] = jnp.zeros_like(halo)

    def short(stream, g):
        rows_of = slice(g * GROUP, (g + 1) * GROUP)
        tiles = [proj_ref[stream, rows_of, b * BLOCK : (b + 1) * BLOCK] for b in range(blocks)]
        before = [halo[stream, rows_of, :]] + tiles[:-1]
        signal = jnp.concatenate(
            [jnp.concatenate(before, axis=0), jnp.concatenate(tiles, axis=0)], axis=1
        )
        return lax.dot_general(
            bands[stream, g], signal, (((1,), (1,)), ((), ())), preferred_element_type=jnp.float32
        )

    for g in range(groups):
        mixed[pl.ds(g, BLOCK, stride=groups), :] = short(1, g) * short(2, g)

    def gather_step(r, states):
        x = mixed[pl.ds(pl.multiple_of(r * groups, groups), groups), :]
        return tuple(d * s + x for d, s in zip(decay, states))

    zero = jnp.zeros((groups, lanes), jnp.float32)
    last = lax.fori_loop(0, BLOCK, gather_step, (zero,) * modes, unroll=16)
    at = iota(zero.shape, 1) // GROUP
    for m in range(modes):
        total, hop = last[m], 1
        while hop < blocks:
            moved = jnp.exp(of_mode(rate_s, m) * (-float(BLOCK * hop))) * pltpu.roll(
                total, GROUP * hop, 1
            )
            total = total + jnp.where(at >= hop, moved, 0.0)
            hop *= 2
        state[m * groups : (m + 1) * groups, :] = total

    end_copies = [
        pltpu.make_async_remote_copy(
            src_ref=state,
            dst_ref=ends.at[hop - 1],
            send_sem=end_send.at[hop - 1],
            recv_sem=end_recv.at[hop - 1],
            device_id={"ctx": (index + hop) % ctx},
            device_id_type=MESH,
        )
        for hop in range(1, ctx)
    ]
    for hop in range(1, ctx):

        @pl.when(index < ctx - hop)
        def _():
            end_copies[hop - 1].start()

    make_bands(0)
    for g in range(groups):
        query[pl.ds(g, BLOCK, stride=groups), :] = short(0, g)
    loads[2].wait()
    loads[3].wait()
    residue_s[...] = spread_rows(residue_ref[...]) * jnp.sqrt(2.0 * rate_s[...] / modes)
    skip_rows = jnp.where(
        iota((groups, width), 1) // GROUP == iota((groups, width), 0),
        jnp.broadcast_to(skip_ref[...], (groups, width)),
        0.0,
    )
    skip = jnp.dot(skip_rows, spread, precision=HIGHEST, preferred_element_type=jnp.float32)
    at_tokens = at.astype(jnp.float32) * float(BLOCK)
    across = [jnp.exp(of_mode(rate_s, m) * (-float(tokens))) for m in range(modes)]
    shift = [jnp.exp(-of_mode(rate_s, m) * at_tokens) for m in range(modes)]

    for hop in range(1, ctx):

        @pl.when(index >= hop)
        def _():
            end_copies[hop - 1].wait_recv()

        @pl.when(index < hop)
        def _():
            ends[hop - 1] = jnp.zeros((high, lanes), jnp.float32)

    entry, weight = [], []
    for m in range(modes):
        incoming = jnp.zeros_like(zero)
        for hop in range(ctx - 1, 0, -1):
            incoming = across[m] * incoming + ends[hop - 1, m * groups : (m + 1) * groups, :]
        incoming = jnp.where(at == blocks - 1, incoming, 0.0)
        hop = 1
        while hop < blocks:
            incoming = incoming + pltpu.roll(incoming, GROUP * hop, 1)
            hop *= 2
        own = jnp.where(at >= 1, pltpu.roll(of_mode(state, m), GROUP, 1), 0.0)
        entry.append(own + shift[m] * incoming)
        weight.append(of_mode(residue_s, m))

    def step(r, states):
        where = pl.ds(pl.multiple_of(r * groups, groups), groups)
        x = mixed[where, :]
        new = tuple(d * s + x for d, s in zip(decay, states))
        parts = [w * s for w, s in zip(weight, new)] + [skip * x]
        while len(parts) > 1:
            parts = [a + b for a, b in zip(parts[::2], parts[1::2])] + (
                [parts[-1]] if len(parts) % 2 else []
            )
        work[where, :] = query[where, :] * parts[0]
        return new

    lax.fori_loop(0, BLOCK, step, tuple(entry), unroll=8)
    per_piece = blocks // PIECES
    for g in range(groups):
        turned = work[pl.ds(g, BLOCK, stride=groups), :].astype(jnp.bfloat16).T
        for b in range(blocks):
            inside = (b % per_piece) * BLOCK
            gath[
                chan, b // per_piece, g * GROUP : (g + 1) * GROUP, inside : inside + BLOCK
            ] = turned[b * GROUP : (b + 1) * GROUP]

    half = chans // 2

    def ring_copy(way, hop, piece):
        shard = ring_chan((place + chans + (-hop if way == 0 else hop)) % chans, chans)
        return pltpu.make_async_remote_copy(
            src_ref=gath.at[shard, piece],
            dst_ref=gath.at[shard, piece],
            send_sem=ring_send.at[way, hop, piece],
            recv_sem=ring_recv.at[way, hop, piece],
            device_id={"chan": right if way == 0 else left},
            device_id_type=MESH,
        )

    def travels(way, hop, piece):
        if hop < half - 1:
            return True
        return hop == half - 1 and (piece < PIECES // 2) == (way == 0)

    copies = {}
    for piece in range(PIECES):
        for way in range(2):
            copies[way, 0, piece] = ring_copy(way, 0, piece)
            copies[way, 0, piece].start()
    weight_copy.wait()

    def project(shard, piece):
        rows_of = pl.ds(pl.multiple_of(shard * width, width), width)
        return lax.dot_general(
            own_weight[rows_of, :],
            gath[shard, piece],
            (((0,), (0,)), ((), ())),
            preferred_element_type=jnp.float32,
        )

    for piece in range(PIECES):
        acc[piece] = project(chan, piece)
    for hop in range(1, half + 1):
        for piece in range(PIECES):
            arrived = []
            for way in range(2):
                if not travels(way, hop - 1, piece):
                    continue
                copies[way, hop - 1, piece].wait_recv()
                if travels(way, hop, piece):
                    copies[way, hop, piece] = ring_copy(way, hop, piece)
                    copies[way, hop, piece].start()
                arrived.append(
                    ring_chan((place + chans + (-hop if way == 0 else hop)) % chans, chans)
                )
            total = acc[piece]
            for shard in arrived:
                total = total + project(shard, piece)
            if hop == half:
                out_ref[:, piece * cols : (piece + 1) * cols] = total.astype(out_ref.dtype)
            else:
                acc[piece] = total

    for key in copies:
        copies[key].wait_send()

    @pl.when(index < ctx - 1)
    def _():
        halo_copy.wait_send()

    for hop in range(1, ctx):

        @pl.when(index < ctx - hop)
        def _():
            end_copies[hop - 1].wait_send()


def per_device(ctx, chans, proj, taps, rate, residue, skip, out_weight):
    width, tokens = proj.shape[1:]
    modes = rate.shape[1]
    groups, blocks = width // GROUP, tokens // BLOCK
    lanes = blocks * GROUP
    if width % 128:
        out_weight = lax.dynamic_slice_in_dim(
            out_weight, lax.axis_index("chan") * width, width, 1
        )
    vmem = pl.BlockSpec(memory_space=pltpu.VMEM)
    major = pltpu.VMEM((BLOCK * groups, lanes), jnp.float32)
    table = pltpu.VMEM((modes * groups, lanes), jnp.float32)
    return pl.pallas_call(
        functools.partial(fused, ctx, chans),
        out_shape=pltpu.VMEM((width, tokens), jnp.bfloat16),
        in_specs=[pl.BlockSpec(memory_space=pltpu.HBM)] * 6,
        out_specs=vmem,
        scratch_shapes=[
            pltpu.VMEM(proj.shape, proj.dtype),
            pltpu.VMEM(taps.shape, taps.dtype),
            pltpu.VMEM((modes, width), jnp.float32),
            pltpu.VMEM((modes, width), jnp.float32),
            pltpu.VMEM((1, width), jnp.float32),
            pltpu.VMEM((3, width, BLOCK), jnp.bfloat16),
            major,
            major,
            major,
            pltpu.VMEM((3, groups, BLOCK, 2 * BLOCK), jnp.bfloat16),
            table,
            table,
            table,
            pltpu.VMEM((ctx - 1, modes * groups, lanes), jnp.float32),
            pltpu.VMEM((chans * width, width), jnp.bfloat16),
            pltpu.VMEM((chans, PIECES, width, tokens // PIECES), jnp.bfloat16),
            pltpu.VMEM((PIECES, width, tokens // PIECES), jnp.float32),
            pltpu.SemaphoreType.DMA,
            pltpu.SemaphoreType.DMA((5,)),
            pltpu.SemaphoreType.DMA((2,)),
            pltpu.SemaphoreType.DMA((ctx - 1,)),
            pltpu.SemaphoreType.DMA((ctx - 1,)),
            pltpu.SemaphoreType.DMA((2, chans // 2, PIECES)),
            pltpu.SemaphoreType.DMA((2, chans // 2, PIECES)),
        ],
        compiler_params=pltpu.CompilerParams(
            vmem_limit_bytes=58 << 20, collective_id=0, has_side_effects=True
        ),
        name="fused",
    )(proj, taps, rate.T, residue.T, skip.reshape(1, width), out_weight)


def solution(mesh):
    in_specs = (P(None, "chan", "ctx"), P(), P("chan", None), P("chan", None), P("chan"), P())
    out_specs = P("chan", "ctx")
    return jax.shard_map(
        functools.partial(per_device, mesh.shape["ctx"], mesh.shape["chan"]),
        mesh=mesh,
        in_specs=in_specs,
        out_specs=out_specs,
        check_vma=False,
    )
```
